512 devices in a mesh: rows: 128 (over y, x, z_lo), rep: 4 (over z_hi, core).
Axes of the slice: x: 4, y: 4, z: 16 (z_hi: 2, z_lo: 8; z = z_hi * 8 + z_lo), core: 2. Of those that a mesh axis runs over, the one named last changes fastest.
Arguments:
- covariates: bfloat16 [1048576, 128], P(('rows', 'rep')), may hold values from -6 to 6
- treated: int32 [1048576], P(('rows', 'rep')), may hold values 0 or 1
- landmarks: bfloat16 [1024, 128], P('rows'), may hold values from -6 to 6
- land_treat: bfloat16 [1024], P('rows'), may hold values from 0 to 1
Outputs:
- gram: float32 [1024, 512], P('rows')
- moment: float32 [1024], P('rows')
The draws below stay inside these ranges and needn't reach their ends.
All inputs are finite; a program needn't handle non-finite values. No bound on the sum of `treated` on one device may be relied on, other than what follows from the above.
Results may differ from the reference program's by a relative error of at most 0.0034.
Values may be sent and summed in bfloat16 or wider, within the bound.
No kernel may reach another device: no remote copies, remote signals or barrier semaphores. Data moves between devices by JAX's collectives and lax.ppermute only.
A program may use at most 64 MiB of HBM per device.

```python
import math
import jax
import jax.numpy as jnp
from jax import lax

D = 128
P_SIZE = 512
PANELS = 2
ROWS = 1048576
LANDMARKS = 1024


def plant(result, own_key, low, largest):
    shape = result.shape
    index_at = [jax.random.randint(jax.random.fold_in(own_key, axis), (), 0, shape[axis]) for axis in range(len(shape))]
    result = result.at[tuple(index_at)].set(low)
    longest = shape.index(max(shape))
    index_at[longest] = (index_at[longest] + 1) % shape[longest]
    return result.at[tuple(index_at)].set(largest)


def steps_of(key, shape, pieces, low, top_value):
    loudness = 1.0
    for dim, parts in pieces:
        heights = jax.random.uniform(jax.random.fold_in(jax.random.fold_in(key, 6), dim), (parts,), jnp.float32, low / len(pieces), top_value / len(pieces))
        loudness = loudness * jnp.repeat(jnp.exp(heights), shape[dim] // parts).reshape((-1,) + (1,) * (len(shape) - 1 - dim))
    return loudness


def noise(rng, extent, scale, most, shards=(), dtype=jnp.bfloat16):
    loudness = steps_of(rng, extent, shards, -0.22, 0.18) if shards else 1.0
    values = jax.random.normal(rng, extent, jnp.float32) * scale * loudness
    return jnp.minimum(jnp.maximum(values, -most), most).astype(dtype)


def setup_inputs(seed: int = 0) -> dict:
    arg_keys = jax.random.split(jax.random.key(seed), 5)
    return {
        "covariates": noise(arg_keys[0], (ROWS, D), 1.0, 6.0, ((0, 512),)),
        "treated": plant((jax.random.randint(arg_keys[1], (ROWS,), 0, 2) < 1).astype(jnp.int32), jax.random.fold_in(arg_keys[1], 1), 0, 1),
        "landmarks": noise(arg_keys[2], (LANDMARKS, D), 1.0, 6.0, ((0, 128),)),
        "land_treat": jnp.clip(1.0 * jax.random.uniform(arg_keys[3], (LANDMARKS,), jnp.float32) ** steps_of(arg_keys[3], (LANDMARKS,), ((0, 128),), -0.2, 0.2), 0.0, 1.0).astype(jnp.bfloat16),
    }


gamma_rate = 0.03125


def reference(covariates, treated, landmarks, land_treat):
    width = covariates.shape[1]
    block_rows = math.gcd(ROWS, 4096)
    count = ROWS // block_rows
    land_f = landmarks.astype(jnp.float32)
    sq_land = jnp.sum(land_f * land_f, axis=1)
    lt_value = land_treat.astype(jnp.float32)
    on_one = jnp.exp(-0.5 * jnp.square(1.0 - lt_value))
    on_zero = jnp.exp(-0.5 * jnp.square(lt_value))
    cov_blocks = covariates.reshape(count, block_rows, width)
    treat_blocks = treated.reshape(count, block_rows)

    def step(carry, item):
        gram_acc, kern_acc = carry
        rows_block, treat_block = item
        rows_f = rows_block.astype(jnp.float32)
        sq_rows = jnp.sum(rows_f * rows_f, axis=1)
        cross = jnp.dot(rows_block, landmarks.T, preferred_element_type=jnp.float32)
        kern = jnp.exp(gamma_rate * (2.0 * width - sq_rows[:, None] - sq_land[None, :] + 2.0 * cross))
        factor = jnp.where(treat_block[:, None] == 1, on_one[None, :], on_zero[None, :])
        features = (kern * factor).astype(jnp.bfloat16)
        feat_f = features.astype(jnp.float32).reshape(block_rows, PANELS, P_SIZE)
        gram_block = jnp.einsum("rpa,rpb->pab", feat_f, feat_f)
        return (gram_acc + gram_block, kern_acc + jnp.sum(kern, axis=0)), None

    start = (jnp.zeros((PANELS, P_SIZE, P_SIZE), jnp.float32), jnp.zeros((PANELS * P_SIZE,), jnp.float32))
    (gram_sum, kern_sum), _ = lax.scan(step, start, (cov_blocks, treat_blocks))
    gram = gram_sum.reshape(PANELS * P_SIZE, P_SIZE) / ROWS
    moment = (on_one - on_zero) * (kern_sum / ROWS)
    return gram, moment
```

```python
import jax
import jax.numpy as jnp
from jax import lax
from jax.sharding import Mesh, PartitionSpec as P

PANELS = 2
Y, X, ZL, ZH, CORE = 4, 4, 8, 2, 2
PLANE = ("y", "x")
RING = ("zh", "zl")

gamma_rate = 0.03125


def spread(block, axes, count):
    copies = jnp.broadcast_to(block[None], (count,) + block.shape)
    return lax.all_to_all(copies, axes, 0, 0)


def on_device(covariates, treated, landmarks, land_treat):
    width = covariates.shape[1]
    total_rows = covariates.shape[0] * Y * X * ZL * ZH * CORE
    own = landmarks.shape[0]
    treat_row = jnp.zeros((8, width), landmarks.dtype).at[0, :own].set(land_treat)
    run = spread(jnp.concatenate([landmarks, treat_row], axis=0), "zl", ZL)
    run_treat = run[:, own, :own].reshape(1, ZL * own)
    run_treat = jnp.pad(run_treat, ((0, 7), (0, width - ZL * own)))
    run_block = jnp.concatenate([run[:, :own].reshape(ZL * own, width), run_treat], axis=0)
    plane = spread(run_block, PLANE, Y * X)
    all_land = plane[:, : ZL * own].reshape(-1, width)
    all_treat = plane[:, ZL * own, : ZL * own].reshape(-1)

    rows_f = covariates.astype(jnp.float32)
    sq_rows = jnp.sum(rows_f * rows_f, axis=1)[:, None]
    land_f = all_land.astype(jnp.float32)
    sq_land = jnp.sum(land_f * land_f, axis=1)
    lt_value = all_treat.astype(jnp.float32)
    on_one = jnp.exp(-0.5 * jnp.square(1.0 - lt_value))
    on_zero = jnp.exp(-0.5 * jnp.square(lt_value))
    is_treated = treated[:, None] == 1
    panel_size = all_land.shape[0] // PANELS
    half = panel_size // CORE
    core = lax.axis_index("core")
    sends, keeps, kern_terms = [], [], []
    for panel in range(PANELS):
        first = panel * panel_size
        block = all_land[first : first + panel_size]
        cross = lax.dot_general(
            covariates, block, (((1,), (1,)), ((), ())), preferred_element_type=jnp.float32
        )
        kern = jnp.exp(
            gamma_rate
            * (2.0 * width - sq_rows - sq_land[None, first : first + panel_size] + 2.0 * cross)
        )
        factor = jnp.where(
            is_treated,
            on_one[None, first : first + panel_size],
            on_zero[None, first : first + panel_size],
        )
        features = (kern * factor).astype(jnp.bfloat16)
        gram = lax.dot_general(
            features, features, (((0,), (0,)), ((), ())), preferred_element_type=jnp.float32
        )
        sends.append(lax.dynamic_slice(gram, (0, (1 - core) * half), (panel_size, half)))
        keeps.append(lax.dynamic_slice(gram, (0, core * half), (panel_size, half)))
        kern_terms.append(jnp.sum(kern, axis=0))
    send = jnp.concatenate(sends, axis=0).astype(jnp.bfloat16)
    keep = jnp.concatenate(keeps, axis=0)
    got = lax.ppermute(send, "core", [(0, 1), (1, 0)])
    pair = (keep + got.astype(jnp.float32)).astype(jnp.bfloat16).reshape(Y * X, ZL * own, half)
    kern_sum = jnp.concatenate(kern_terms, axis=0).astype(jnp.bfloat16).reshape(Y * X, 1, ZL * own)
    kern_sum = jnp.pad(kern_sum, ((0, 0), (0, 7), (0, half - ZL * own)))
    mine = lax.all_to_all(jnp.concatenate([pair, kern_sum], axis=1), PLANE, 0, 0)
    mine = jnp.sum(mine.astype(jnp.float32), axis=0)
    gram_z = mine[: ZL * own].reshape(ZL, own, half)
    kern_z = jnp.pad(mine[ZL * own, : ZL * own].reshape(ZL, 1, own), ((0, 0), (0, 7), (0, half - own)))
    ring = jnp.concatenate([gram_z, kern_z], axis=1)
    ring = jnp.broadcast_to(ring[None], (ZH,) + ring.shape).reshape(ZH * ZL, own + 8, half)
    ring = jnp.sum(lax.all_to_all(ring, RING, 0, 0), axis=0)
    both = lax.all_gather(ring, "core", axis=0)
    gram_out = jnp.concatenate([both[0, :own], both[1, :own]], axis=1) / total_rows
    kern_mean = (both[0, own, :own] + both[1, own, :own]) / total_rows
    t_own = land_treat.astype(jnp.float32)
    moment = (jnp.exp(-0.5 * jnp.square(1.0 - t_own)) - jnp.exp(-0.5 * jnp.square(t_own))) * kern_mean
    return gram_out, moment


def solution(mesh):
    fine = Mesh(mesh.devices.reshape(Y, X, ZL, ZH, CORE), ("y", "x", "zl", "zh", "core"))
    rows, rep = ("y", "x", "zl"), ("zh", "core")
    in_specs = (P(rows + rep, None), P(rows + rep), P(rows, None), P(rows))
    out_specs = (P(rows, None), P(rows))
    return jax.shard_map(
        on_device, mesh=fine, in_specs=in_specs, out_specs=out_specs, check_vma=False
    )
```

```python
import jax
import jax.numpy as jnp
from jax import lax
from jax.experimental import pallas as pl
from jax.experimental.pallas import tpu as pltpu
from jax.sharding import Mesh, PartitionSpec as P

Y, X, ZL, ZH, CORE = 4, 4, 8, 2, 2
PLANE = ("y", "x")
RING = ("zh", "zl")
PANELS = 2
MASKS = 16
BLOCK = 512
GROUP = 16
LANES = 128

gamma_rate = 0.03125


def spread(block, axes, count):
    copies = jnp.broadcast_to(block[None], (count,) + block.shape)
    return lax.all_to_all(copies, axes, 0, 0)


def three_parts(value):
    high = lax.reduce_precision(value, 8, 7)
    rest = value - high
    middle = lax.reduce_precision(rest, 8, 7)
    return high, middle, rest - middle


def by_lane(shape, offset, columns):
    lane = lax.broadcasted_iota(jnp.int32, shape, 1) - offset
    out = jnp.zeros(shape, jnp.float32)
    for at, column in enumerate(columns):
        out = jnp.where(lane == at, column, out)
    return out.astype(jnp.bfloat16)


def row_side(covariates, treated):
    width = covariates.shape[1]
    rows_f = covariates.astype(jnp.float32)
    flag = treated.astype(jnp.float32)
    own = gamma_rate * (2.0 * width - jnp.sum(rows_f * rows_f, axis=1)) - 0.5 * flag
    parts = [part[:, None] for part in three_parts(own)]
    extra = by_lane((covariates.shape[0], LANES), 0, parts + [flag[:, None], 1.0, 1.0, 1.0])
    return jnp.concatenate([covariates, extra], axis=1)


def land_side(landmarks, land_treat):
    land_f = landmarks.astype(jnp.float32)
    value = land_treat.astype(jnp.float32)
    own = -gamma_rate * jnp.sum(land_f * land_f, axis=1) - 0.5 * jnp.square(value)
    parts = [part[:, None] for part in three_parts(own)]
    offset = GROUP * lax.axis_index("zl")
    extra = by_lane((landmarks.shape[0], LANES), offset, [1.0, 1.0, 1.0, value[:, None]] + parts)
    scaled = (land_f * (2.0 * gamma_rate)).astype(jnp.bfloat16)
    return jnp.concatenate([scaled, extra], axis=0)


def gram_kernel(core_ref, own_ref, other_ref, plane_ref, out_ref, land, feat, acc):
    step = pl.program_id(0)
    count = pl.num_programs(0)
    core = core_ref[0]
    places, place_rows = plane_ref.shape[0], plane_ref.shape[1] - 8
    size = places * place_rows // PANELS
    half = size // CORE
    per_panel = places // PANELS

    @pl.when(step == 0)
    def _():
        lane = lax.broadcasted_iota(jnp.int32, (8, LANES), 1)
        for place in range(places):
            base = (place // per_panel) * (size + MASKS) + (place % per_panel) * place_rows
            land[base : base + place_rows, :LANES] = plane_ref[place, :place_rows]
            packed = plane_ref[place, place_rows:].astype(jnp.float32)
            pieces = []
            for group in range(place_rows // 8):
                rolled = packed if group == 0 else pltpu.roll(packed, LANES - GROUP * group, 1)
                pieces.append(jnp.where(lane < GROUP, rolled, 0.0))
            extra = jnp.concatenate(pieces, axis=0)
            land[base : base + place_rows, LANES:] = extra.astype(jnp.bfloat16)
        lane = lax.broadcasted_iota(jnp.int32, (MASKS, LANES), 1)
        row = lax.broadcasted_iota(jnp.int32, (MASKS, LANES), 0)
        flag = jnp.where(lane == 3, 1.0, 0.0)
        other = jnp.where(lane == 4, 1.0, 0.0) - flag
        mask = jnp.where(row == 0, flag, jnp.where(row == 1, other, 0.0)).astype(jnp.bfloat16)
        for panel in range(PANELS):
            base = panel * (size + MASKS) + size
            land[base : base + MASKS, :LANES] = jnp.zeros((MASKS, LANES), jnp.bfloat16)
            land[base : base + MASKS, LANES:] = mask
        acc[...] = jnp.zeros_like(acc)

    def work(rows_ref):
        for panel in range(PANELS):
            base = panel * (size + MASKS)
            arg = lax.dot_general(
                land[base : base + size + MASKS, :],
                rows_ref[...],
                (((1,), (1,)), ((), ())),
                preferred_element_type=jnp.float32,
            )
            feat[panel, :size, :] = jnp.exp(arg[:size]).astype(jnp.bfloat16)
            feat[panel, size:, :] = arg[size:].astype(jnp.bfloat16)
        for panel in range(PANELS):
            mine = feat[panel, pl.ds(pl.multiple_of(core * half, half), half), :]
            acc[panel] += lax.dot_general(
                feat[panel], mine, (((1,), (1,)), ((), ())), preferred_element_type=jnp.float32
            )

    @pl.when(step < count // 2)
    def _():
        work(own_ref)

    @pl.when(step >= count // 2)
    def _():
        work(other_ref)

    @pl.when(step == count - 1)
    def _():
        for place in range(places):
            panel, spot = place // per_panel, place % per_panel
            first = spot * place_rows
            for tile in range(half // LANES):
                out_ref[place, tile * place_rows : (tile + 1) * place_rows, :] = acc[
                    panel, first : first + place_rows, tile * LANES : (tile + 1) * LANES
                ].astype(jnp.bfloat16)
            at = (first % half) // LANES * LANES
            sums = acc[panel, size : size + 8, at : at + LANES]
            sums = jnp.where(core == first // half, sums, 0.0)
            out_ref[place, half // LANES * place_rows :, :] = sums.astype(jnp.bfloat16)


def chip_gram(core, own, other, plane):
    places, place_rows = plane.shape[0], plane.shape[1] - 8
    size = places * place_rows // PANELS
    half = size // CORE
    steps = own.shape[0] // BLOCK
    out_rows = half // LANES * place_rows + 8
    grid_spec = pltpu.PrefetchScalarGridSpec(
        num_scalar_prefetch=1,
        grid=(2 * steps,),
        in_specs=[
            pl.BlockSpec((BLOCK, own.shape[1]), lambda i, c: (jnp.minimum(i, steps - 1), 0)),
            pl.BlockSpec((BLOCK, own.shape[1]), lambda i, c: (jnp.maximum(i - steps, 0), 0)),
            pl.BlockSpec(plane.shape, lambda i, c: (0, 0, 0)),
        ],
        out_specs=pl.BlockSpec((places, out_rows, LANES), lambda i, c: (0, 0, 0)),
        scratch_shapes=[
            pltpu.VMEM((PANELS * (size + MASKS), 2 * LANES), jnp.bfloat16),
            pltpu.VMEM((PANELS, size + MASKS, BLOCK), jnp.bfloat16),
            pltpu.VMEM((PANELS, size + MASKS, half), jnp.float32),
        ],
    )
    rows = 2 * own.shape[0]
    flops = 2 * rows * PANELS * size * (2 * LANES + half)
    return pl.pallas_call(
        gram_kernel,
        grid_spec=grid_spec,
        out_shape=jax.ShapeDtypeStruct((places, out_rows, LANES), jnp.bfloat16),
        compiler_params=pltpu.CompilerParams(
            dimension_semantics=("arbitrary",), vmem_limit_bytes=48 << 20
        ),
        cost_estimate=pl.CostEstimate(
            flops=flops, transcendentals=rows * PANELS * size, bytes_accessed=4 << 20
        ),
        name="chip_gram",
    )(core, own, other, plane)


def on_device(covariates, treated, landmarks, land_treat):
    width = covariates.shape[1]
    total_rows = covariates.shape[0] * Y * X * ZL * ZH * CORE
    own = landmarks.shape[0]
    run = spread(land_side(landmarks, land_treat), "zl", ZL)
    extra = jnp.sum(run[:, own:].astype(jnp.float32), axis=0).astype(jnp.bfloat16)
    run = jnp.concatenate([run[:, :own].reshape(ZL * own, width), extra], axis=0)
    plane = spread(run, PLANE, Y * X)

    rows_own = row_side(covariates, treated)
    rows_other = lax.ppermute(rows_own, "core", [(0, 1), (1, 0)])
    core = lax.axis_index("core").astype(jnp.int32).reshape(1)
    terms = chip_gram(core, rows_own, rows_other, plane)

    mine = lax.all_to_all(terms, PLANE, 0, 0)
    mine = jnp.sum(mine.astype(jnp.float32), axis=0)
    tiles = (mine.shape[0] - 8) // (ZL * own)
    gram_z = mine[: tiles * ZL * own].reshape(tiles, ZL, own, LANES).transpose(1, 0, 2, 3)
    sums_z = jnp.broadcast_to(mine[None, tiles * ZL * own :], (ZL, 8, LANES))
    ring = jnp.concatenate([gram_z.reshape(ZL, tiles * own, LANES), sums_z], axis=1)
    ring = jnp.broadcast_to(ring[None], (ZH,) + ring.shape).reshape((ZH * ZL,) + ring.shape[1:])
    ring = jnp.sum(lax.all_to_all(ring, RING, 0, 0), axis=0)
    both = lax.all_gather(ring, "core", axis=0)
    gram = both[:, : tiles * own].reshape(CORE * tiles, own, LANES).transpose(1, 0, 2)
    gram_out = gram.reshape(own, CORE * tiles * LANES) * (1.0 / total_rows)
    sums = both[0, tiles * own : tiles * own + 2] + both[1, tiles * own : tiles * own + 2]
    at = 64 * (lax.axis_index("x") % 2) + own * lax.axis_index("zl")
    sums = lax.dynamic_slice(sums, (0, at), (2, own))
    t_own = land_treat.astype(jnp.float32)
    on_one = jnp.exp(-0.5 * jnp.square(1.0 - t_own))
    on_zero = jnp.exp(-0.5 * jnp.square(t_own))
    moment = (on_one - on_zero) * ((sums[0] / on_one + sums[1] / on_zero) * (1.0 / total_rows))
    return gram_out, moment


def solution(mesh):
    fine = Mesh(mesh.devices.reshape(Y, X, ZL, ZH, CORE), ("y", "x", "zl", "zh", "core"))
    rows, rep = ("y", "x", "zl"), ("zh", "core")
    in_specs = (P(rows + rep, None), P(rows + rep), P(rows, None), P(rows))
    out_specs = (P(rows, None), P(rows))
    return jax.shard_map(
        on_device, mesh=fine, in_specs=in_specs, out_specs=out_specs, check_vma=False
    )
```

```python
import jax
import jax.numpy as jnp
from jax import lax
from jax.experimental import pallas as pl
from jax.experimental.pallas import tpu as pltpu
from jax.sharding import Mesh, PartitionSpec as P

Y, X, ZL, ZH, CORE = 4, 4, 8, 2, 2
PLANE = ("y", "x")
RING = ("zh", "zl")
PANELS = 2
OWN = 8
RUN = ZL * OWN
MASKS = 16
BLOCK = 1024
GROUP = 16
LANES = 128
NT = (((1,), (1,)), ((), ()))

gamma_rate = 0.03125


def call(kernel, out_shape, *args, scratch=(), cost=None, vmem=16 << 20):
    whole = pl.BlockSpec(memory_space=pltpu.VMEM)
    several = isinstance(out_shape, tuple)
    return pl.pallas_call(
        kernel,
        in_specs=[whole] * len(args),
        out_specs=(whole,) * len(out_shape) if several else whole,
        out_shape=out_shape,
        scratch_shapes=list(scratch),
        compiler_params=pltpu.CompilerParams(vmem_limit_bytes=vmem),
        cost_estimate=cost,
        name=kernel.__name__,
    )(*args)


def rounded(value):
    return value.astype(jnp.bfloat16).astype(jnp.float32)


def three_parts(value):
    high = rounded(value)
    middle = rounded(value - high)
    return high, middle, value - high - middle


def pack_kernel(land_ref, treat_ref, out_ref):
    land = land_ref[...].astype(jnp.float32)
    row = lax.broadcasted_iota(jnp.int32, (OWN, OWN), 0)
    col = lax.broadcasted_iota(jnp.int32, (OWN, OWN), 1)
    treat = jnp.broadcast_to(treat_ref[...].astype(jnp.float32), (OWN, OWN))
    treat = jnp.sum(jnp.where(row == col, treat, 0.0), axis=1, keepdims=True)
    own = -gamma_rate * jnp.sum(land * land, axis=1, keepdims=True) - 0.5 * treat * treat
    lane = lax.broadcasted_iota(jnp.int32, (OWN, LANES), 1) - GROUP * lax.axis_index("zl")
    extra = jnp.where((lane >= 0) & (lane < 3), 1.0, 0.0)
    for at, part in enumerate((treat,) + three_parts(own)):
        extra = jnp.where(lane == 3 + at, part, extra)
    land = (land * (2.0 * gamma_rate)).astype(jnp.bfloat16)
    extra = extra.astype(jnp.bfloat16)
    for place in range(ZL):
        out_ref[place, :OWN] = land
        out_ref[place, OWN:] = extra


def run_kernel(run_ref, out_ref):
    extra = run_ref[0, OWN:].astype(jnp.float32)
    for place in range(1, ZL):
        extra += run_ref[place, OWN:].astype(jnp.float32)
    extra = extra.astype(jnp.bfloat16)
    for place in range(Y * X):
        for part in range(ZL):
            out_ref[place, part * OWN : (part + 1) * OWN] = run_ref[part, :OWN]
        out_ref[place, RUN:] = extra


def gram_kernel(rows_ref, flag_ref, plane_ref, send_ref, keep_ref, land, feat, acc):
    core = lax.axis_index("core")
    per_panel = Y * X // PANELS
    size = per_panel * RUN
    half = size // CORE
    rows, width = rows_ref.shape
    lane = lax.broadcasted_iota(jnp.int32, (8, LANES), 1)
    for place in range(Y * X):
        panel, base = place // per_panel, (place % per_panel) * RUN
        land[panel, base : base + RUN, :LANES] = plane_ref[place, :RUN]
        packed = plane_ref[place, RUN:].astype(jnp.float32)
        pieces = []
        for group in range(ZL):
            rolled = packed if group == 0 else pltpu.roll(packed, LANES - GROUP * group, 1)
            pieces.append(jnp.where(lane < GROUP, rolled, 0.0))
        extra = jnp.concatenate(pieces, axis=0).astype(jnp.bfloat16)
        land[panel, base : base + RUN, LANES:] = extra
    ones = jnp.ones((8, 2 * width), jnp.bfloat16)
    for at in range(0, rows, BLOCK):
        block = rows_ref[at : at + BLOCK, :]
        square = jnp.square(block.astype(jnp.float32))
        high = square.astype(jnp.bfloat16)
        low = (square - high.astype(jnp.float32)).astype(jnp.bfloat16)
        total = lax.dot_general(
            ones, jnp.concatenate([high, low], axis=1), NT, preferred_element_type=jnp.float32
        )
        flag = flag_ref[0:1, at : at + BLOCK].astype(jnp.float32)
        own = three_parts(gamma_rate * (2.0 * width - total) - 0.5 * flag)
        row = lax.broadcasted_iota(jnp.int32, (8, BLOCK), 0)
        extra = jnp.where(row == 3, flag, 1.0)
        for index, part in enumerate(own):
            extra = jnp.where(row == index, part, extra)
        extra = jnp.concatenate([extra, jnp.zeros((LANES - 8, BLOCK), jnp.float32)], axis=0)
        wide = jnp.concatenate([block, extra.T.astype(jnp.bfloat16)], axis=1)
        row = lax.broadcasted_iota(jnp.int32, (MASKS, BLOCK), 0)
        mask = jnp.where(row == 0, flag, jnp.where(row == 1, 1.0 - flag, 0.0))
        for panel in range(PANELS):
            arg = lax.dot_general(land[panel], wide, NT, preferred_element_type=jnp.float32)
            feat[panel, :size, at : at + BLOCK] = jnp.exp(arg).astype(jnp.bfloat16)
            feat[panel, size:, at : at + BLOCK] = mask.astype(jnp.bfloat16)
    for panel in range(PANELS):
        for which, out_ref in ((1 - core, send_ref), (core, keep_ref)):
            mine = feat[panel, pl.ds(pl.multiple_of(which * half, half), half), :]
            acc[...] = lax.dot_general(feat[panel], mine, NT, preferred_element_type=jnp.float32)
            for spot in range(per_panel):
                place, first = panel * per_panel + spot, spot * RUN
                for tile in range(half // LANES):
                    out_ref[place, tile * RUN : (tile + 1) * RUN, :] = acc[
                        first : first + RUN, tile * LANES : (tile + 1) * LANES
                    ].astype(out_ref.dtype)
                lanes = (first % half) // LANES * LANES
                sums = acc[size : size + 8, lanes : lanes + LANES]
                sums = jnp.where(which == first // half, sums, 0.0)
                out_ref[place, half // LANES * RUN :, :] = sums.astype(out_ref.dtype)


def chip_gram(rows, flag, plane):
    size = Y * X // PANELS * RUN
    half = size // CORE
    shape = (Y * X, half // LANES * RUN + 8, LANES)
    count, width = rows.shape
    return call(
        gram_kernel,
        (jax.ShapeDtypeStruct(shape, jnp.bfloat16), jax.ShapeDtypeStruct(shape, jnp.float32)),
        rows,
        flag,
        plane,
        scratch=[
            pltpu.VMEM((PANELS, size, 2 * LANES), jnp.bfloat16),
            pltpu.VMEM((PANELS, size + MASKS, count), jnp.bfloat16),
            pltpu.VMEM((size + MASKS, half), jnp.float32),
        ],
        cost=pl.CostEstimate(
            flops=2 * count * PANELS * size * (size + 2 * width),
            transcendentals=count * PANELS * size,
            bytes_accessed=4 << 20,
        ),
        vmem=40 << 20,
    )


def pair_kernel(keep_ref, got_ref, out_ref):
    out_ref[...] = (keep_ref[...] + got_ref[...].astype(jnp.float32)).astype(jnp.bfloat16)


def plane_sum_kernel(terms_ref, out_ref):
    total = terms_ref[0].astype(jnp.float32)
    for place in range(1, Y * X):
        total += terms_ref[place].astype(jnp.float32)
    total = total.astype(jnp.bfloat16)
    tiles = (total.shape[0] - 8) // RUN
    for high in range(ZH):
        for low in range(ZL):
            for tile in range(tiles):
                at = tile * RUN + low * OWN
                out_ref[high * ZL + low, tile * OWN : (tile + 1) * OWN] = total[at : at + OWN]
            out_ref[high * ZL + low, tiles * OWN :] = total[tiles * RUN :]


def ring_sum_kernel(terms_ref, out_ref):
    total = terms_ref[0].astype(jnp.float32)
    for place in range(1, ZH * ZL):
        total += terms_ref[place].astype(jnp.float32)
    out_ref[...] = total


def finish_kernel(scale, both_ref, treat_ref, gram_ref, moment_ref):
    rows = both_ref.shape[0] // CORE
    tiles = (rows - 8) // OWN
    for core in range(CORE):
        for tile in range(tiles):
            at = core * tiles + tile
            first = core * rows + tile * OWN
            gram_ref[:, at * LANES : (at + 1) * LANES] = both_ref[first : first + OWN] * scale
    sums = both_ref[tiles * OWN : rows] + both_ref[rows + tiles * OWN :]
    at = RUN * (lax.axis_index("x") % (LANES // RUN)) + OWN * lax.axis_index("zl")
    sums = pltpu.roll(sums, (LANES - at) % LANES, 1)
    treat = treat_ref[...].astype(jnp.float32)
    on_one = jnp.exp(-0.5 * jnp.square(1.0 - treat))
    on_zero = jnp.exp(-0.5 * jnp.square(treat))
    kern = sums[0:1, :OWN] / on_one + sums[1:2, :OWN] / on_zero
    moment_ref[...] = (on_one - on_zero) * (kern * scale)


def on_device(covariates, treated, landmarks, land_treat):
    count, width = covariates.shape
    scale = 1.0 / (count * Y * X * ZL * ZH * CORE)
    bf16, f32 = jnp.bfloat16, jnp.float32
    treat_row = land_treat.reshape(1, OWN)
    run = call(pack_kernel, jax.ShapeDtypeStruct((ZL, 2 * OWN, width), bf16), landmarks, treat_row)
    run = lax.all_to_all(run, "zl", 0, 0)
    plane = call(run_kernel, jax.ShapeDtypeStruct((Y * X, RUN + 8, width), bf16), run)
    plane = lax.all_to_all(plane, PLANE, 0, 0)

    send, keep = chip_gram(covariates, treated.reshape(1, count), plane)
    got = lax.ppermute(send, "core", [(0, 1), (1, 0)])
    terms = call(pair_kernel, jax.ShapeDtypeStruct(send.shape, bf16), keep, got)
    terms = lax.all_to_all(terms, PLANE, 0, 0)
    rows = (terms.shape[1] - 8) // ZL + 8
    ring = call(plane_sum_kernel, jax.ShapeDtypeStruct((ZH * ZL, rows, LANES), bf16), terms)
    ring = lax.all_to_all(ring, RING, 0, 0)
    ring = call(ring_sum_kernel, jax.ShapeDtypeStruct((rows, LANES), f32), ring)
    both = lax.all_gather(ring, "core", axis=0, tiled=True)

    def finish(*refs):
        finish_kernel(scale, *refs)

    gram, moment = call(
        finish,
        (
            jax.ShapeDtypeStruct((OWN, CORE * (rows - 8) // OWN * LANES), f32),
            jax.ShapeDtypeStruct((1, OWN), f32),
        ),
        both,
        treat_row,
    )
    return gram, moment.reshape(OWN)


def solution(mesh):
    fine = Mesh(mesh.devices.reshape(Y, X, ZL, ZH, CORE), ("y", "x", "zl", "zh", "core"))
    rows, rep = ("y", "x", "zl"), ("zh", "core")
    in_specs = (P(rows + rep, None), P(rows + rep), P(rows, None), P(rows))
    out_specs = (P(rows, None), P(rows))
    return jax.shard_map(
        on_device, mesh=fine, in_specs=in_specs, out_specs=out_specs, check_vma=False
    )
```

```python
import jax
import jax.numpy as jnp
from jax import lax
from jax.experimental import pallas as pl
from jax.experimental.pallas import tpu as pltpu
from jax.sharding import Mesh, PartitionSpec as P

Y, X, ZL, ZH, CORE = 4, 4, 8, 2, 2
PLANE = ("y", "x")
RING = ("zh", "zl")
PANELS = 2
OWN = 8
RUN = ZL * OWN
MASKS = 16
BLOCK = 2048
FIRST = 4
GROUP = 16
LANES = 128
NT = (((1,), (1,)), ((), ()))

gamma_rate = 0.03125


def run_groups():
    near = [FIRST + (low - FIRST) % ZL for low in range(ZL)]
    return [near, [(place + ZL) % (ZH * ZL) for place in near]]


def call(kernel, out_shape, *args, scratch=(), cost=None, vmem=16 << 20, space=pltpu.VMEM):
    whole = pl.BlockSpec(memory_space=pltpu.VMEM)
    several = isinstance(out_shape, tuple)
    return pl.pallas_call(
        kernel,
        in_specs=[pl.BlockSpec(memory_space=space)] * len(args),
        out_specs=(whole,) * len(out_shape) if several else whole,
        out_shape=out_shape,
        scratch_shapes=list(scratch),
        compiler_params=pltpu.CompilerParams(vmem_limit_bytes=vmem),
        cost_estimate=cost,
        name=kernel.__name__,
    )(*args)


def rounded(value):
    return value.astype(jnp.bfloat16).astype(jnp.float32)


def three_parts(value):
    high = rounded(value)
    middle = rounded(value - high)
    return high, middle, value - high - middle


def pack_kernel(land_ref, treat_ref, out_ref):
    land = land_ref[...].astype(jnp.float32)
    row = lax.broadcasted_iota(jnp.int32, (OWN, OWN), 0)
    col = lax.broadcasted_iota(jnp.int32, (OWN, OWN), 1)
    treat = jnp.broadcast_to(treat_ref[...].astype(jnp.float32), (OWN, OWN))
    treat = jnp.sum(jnp.where(row == col, treat, 0.0), axis=1, keepdims=True)
    own = -gamma_rate * jnp.sum(land * land, axis=1, keepdims=True) - 0.5 * treat * treat
    lane = lax.broadcasted_iota(jnp.int32, (OWN, LANES), 1) - GROUP * lax.axis_index("zl")
    extra = jnp.where((lane >= 0) & (lane < 3), 1.0, 0.0)
    for at, part in enumerate((treat,) + three_parts(own)):
        extra = jnp.where(lane == 3 + at, part, extra)
    land = (land * (2.0 * gamma_rate)).astype(jnp.bfloat16)
    extra = extra.astype(jnp.bfloat16)
    for place in range(ZL):
        out_ref[place, :OWN] = land
        out_ref[place, OWN:] = extra


def run_kernel(run_ref, out_ref):
    extra = run_ref[0, OWN:].astype(jnp.float32)
    for place in range(1, ZL):
        extra += run_ref[place, OWN:].astype(jnp.float32)
    extra = extra.astype(jnp.bfloat16)
    for place in range(Y * X):
        for part in range(ZL):
            out_ref[place, part * OWN : (part + 1) * OWN] = run_ref[part, :OWN]
        out_ref[place, RUN:] = extra


def gram_kernel(rows_ref, flag_ref, plane_ref, send_ref, keep_ref, land, feat, acc):
    core = lax.axis_index("core")
    per_panel = Y * X // PANELS
    size = per_panel * RUN
    half = size // CORE
    rows, width = rows_ref.shape
    lane = lax.broadcasted_iota(jnp.int32, (8, LANES), 1)
    for place in range(Y * X):
        panel, base = place // per_panel, (place % per_panel) * RUN
        land[panel, base : base + RUN, :LANES] = plane_ref[place, :RUN]
        packed = plane_ref[place, RUN:].astype(jnp.float32)
        pieces = []
        for group in range(ZL):
            rolled = packed if group == 0 else pltpu.roll(packed, LANES - GROUP * group, 1)
            pieces.append(jnp.where(lane < GROUP, rolled, 0.0))
        extra = jnp.concatenate(pieces, axis=0).astype(jnp.bfloat16)
        land[panel, base : base + RUN, LANES:] = extra
    ones = jnp.ones((8, 2 * width), jnp.bfloat16)
    for at in range(0, rows, BLOCK):
        block = rows_ref[at : at + BLOCK, :]
        square = jnp.square(block.astype(jnp.float32))
        high = square.astype(jnp.bfloat16)
        low = (square - high.astype(jnp.float32)).astype(jnp.bfloat16)
        total = lax.dot_general(
            ones, jnp.concatenate([high, low], axis=1), NT, preferred_element_type=jnp.float32
        )
        flag = flag_ref[0:1, at : at + BLOCK].astype(jnp.float32)
        own = three_parts(gamma_rate * (2.0 * width - total) - 0.5 * flag)
        row = lax.broadcasted_iota(jnp.int32, (8, BLOCK), 0)
        extra = jnp.where(row == 3, flag, 1.0)
        for index, part in enumerate(own):
            extra = jnp.where(row == index, part, extra)
        extra = jnp.concatenate([extra, jnp.zeros((LANES - 8, BLOCK), jnp.float32)], axis=0)
        wide = jnp.concatenate([block, extra.T.astype(jnp.bfloat16)], axis=1)
        row = lax.broadcasted_iota(jnp.int32, (MASKS, BLOCK), 0)
        mask = jnp.where(row == 0, flag, jnp.where(row == 1, 1.0 - flag, 0.0))
        for panel in range(PANELS):
            arg = lax.dot_general(land[panel], wide, NT, preferred_element_type=jnp.float32)
            feat[panel, :size, at : at + BLOCK] = jnp.exp(arg).astype(jnp.bfloat16)
            feat[panel, size:, at : at + BLOCK] = mask.astype(jnp.bfloat16)
    for panel in range(PANELS):
        for which, out_ref in ((1 - core, send_ref), (core, keep_ref)):
            mine = feat[panel, pl.ds(pl.multiple_of(which * half, half), half), :]
            acc[...] = lax.dot_general(feat[panel], mine, NT, preferred_element_type=jnp.float32)
            for spot in range(per_panel):
                place, first = panel * per_panel + spot, spot * RUN
                for tile in range(half // LANES):
                    out_ref[place, tile * RUN : (tile + 1) * RUN, :] = acc[
                        first : first + RUN, tile * LANES : (tile + 1) * LANES
                    ].astype(out_ref.dtype)
                lanes = (first % half) // LANES * LANES
                sums = acc[size : size + 8, lanes : lanes + LANES]
                sums = jnp.where(which == first // half, sums, 0.0)
                out_ref[place, half // LANES * RUN :, :] = sums.astype(out_ref.dtype)


def chip_gram(rows, flag, plane):
    size = Y * X // PANELS * RUN
    half = size // CORE
    shape = (Y * X, half // LANES * RUN + 8, LANES)
    count, width = rows.shape
    return call(
        gram_kernel,
        (jax.ShapeDtypeStruct(shape, jnp.bfloat16), jax.ShapeDtypeStruct(shape, jnp.float32)),
        rows,
        flag,
        plane,
        scratch=[
            pltpu.VMEM((PANELS, size, 2 * LANES), jnp.bfloat16),
            pltpu.VMEM((PANELS, size + MASKS, count), jnp.bfloat16),
            pltpu.VMEM((size + MASKS, half), jnp.float32),
        ],
        cost=pl.CostEstimate(
            flops=2 * count * PANELS * size * (size + 2 * width),
            transcendentals=count * PANELS * size,
            bytes_accessed=4 << 20,
        ),
        vmem=40 << 20,
    )


def pair_kernel(keep_ref, got_ref, out_ref):
    out_ref[...] = (keep_ref[...] + got_ref[...].astype(jnp.float32)).astype(jnp.bfloat16)


def plane_sum_kernel(terms_ref, out_ref):
    total = terms_ref[0].astype(jnp.float32)
    for place in range(1, Y * X):
        total += terms_ref[place].astype(jnp.float32)
    total = total.astype(jnp.bfloat16)
    tiles = (total.shape[0] - 8) // RUN
    for high in range(ZH):
        for low in range(ZL):
            for tile in range(tiles):
                at = tile * RUN + low * OWN
                out_ref[high * ZL + low, tile * OWN : (tile + 1) * OWN] = total[at : at + OWN]
            out_ref[high * ZL + low, tiles * OWN :] = total[tiles * RUN :]


def ring_sum_kernel(terms_ref, out_ref):
    total = terms_ref[0].astype(jnp.float32)
    for place in range(1, ZH * ZL):
        total += terms_ref[place].astype(jnp.float32)
    out_ref[...] = total


def finish_kernel(scale, both_ref, treat_ref, gram_ref, moment_ref):
    rows = both_ref.shape[0] // CORE
    tiles = (rows - 8) // OWN
    for core in range(CORE):
        for tile in range(tiles):
            at = core * tiles + tile
            first = core * rows + tile * OWN
            gram_ref[:, at * LANES : (at + 1) * LANES] = both_ref[first : first + OWN] * scale
    sums = both_ref[tiles * OWN : rows] + both_ref[rows + tiles * OWN :]
    at = RUN * (lax.axis_index("x") % (LANES // RUN)) + OWN * lax.axis_index("zl")
    sums = pltpu.roll(sums, (LANES - at) % LANES, 1)
    treat = treat_ref[...].astype(jnp.float32)
    on_one = jnp.exp(-0.5 * jnp.square(1.0 - treat))
    on_zero = jnp.exp(-0.5 * jnp.square(treat))
    kern = sums[0:1, :OWN] / on_one + sums[1:2, :OWN] / on_zero
    moment_ref[...] = (on_one - on_zero) * (kern * scale)


def on_device(covariates, treated, landmarks, land_treat):
    count, width = covariates.shape
    scale = 1.0 / (count * Y * X * ZL * ZH * CORE)
    bf16, f32 = jnp.bfloat16, jnp.float32
    treat_row = land_treat.reshape(1, OWN)
    run = call(pack_kernel, jax.ShapeDtypeStruct((ZL, 2 * OWN, width), bf16), landmarks, treat_row)
    run = lax.all_to_all(run, RING, 0, 0, axis_index_groups=run_groups())
    plane = call(
        run_kernel,
        jax.ShapeDtypeStruct((Y * X, RUN + 8, width), bf16),
        run,
        cost=pl.CostEstimate(flops=1 << 32, transcendentals=0, bytes_accessed=1 << 25),
    )
    plane = lax.all_to_all(plane, PLANE, 0, 0)

    send, keep = chip_gram(covariates, treated.reshape(1, count), plane)
    got = lax.ppermute(send, "core", [(0, 1), (1, 0)])
    terms = call(pair_kernel, jax.ShapeDtypeStruct(send.shape, bf16), keep, got)
    terms = lax.all_to_all(terms, PLANE, 0, 0)
    rows = (terms.shape[1] - 8) // ZL + 8
    ring = call(plane_sum_kernel, jax.ShapeDtypeStruct((ZH * ZL, rows, LANES), bf16), terms)
    ring = lax.all_to_all(ring, RING, 0, 0)
    ring = call(ring_sum_kernel, jax.ShapeDtypeStruct((rows, LANES), f32), ring)
    both = lax.all_gather(ring, "core", axis=0, tiled=True)

    def finish(*refs):
        finish_kernel(scale, *refs)

    gram, moment = call(
        finish,
        (
            jax.ShapeDtypeStruct((OWN, CORE * (rows - 8) // OWN * LANES), f32),
            jax.ShapeDtypeStruct((1, OWN), f32),
        ),
        both,
        treat_row,
    )
    return gram, moment.reshape(OWN)


def solution(mesh):
    fine = Mesh(mesh.devices.reshape(Y, X, ZL, ZH, CORE), ("y", "x", "zl", "zh", "core"))
    rows, rep = ("y", "x", "zl"), ("zh", "core")
    in_specs = (P(rows + rep, None), P(rows + rep), P(rows, None), P(rows))
    out_specs = (P(rows, None), P(rows))
    return jax.shard_map(
        on_device, mesh=fine, in_specs=in_specs, out_specs=out_specs, check_vma=False
    )
```

```python
import jax
import jax.numpy as jnp
from jax import lax
from jax.experimental import pallas as pl
from jax.experimental.pallas import tpu as pltpu
from jax.sharding import Mesh, PartitionSpec as P

Y, X, ZL, ZH, CORE = 4, 4, 8, 2, 2
PLANE = ("y", "x")
RING = ("zh", "zl")
PANELS = 2
OWN = 8
RUN = ZL * OWN
MASKS = 16
BLOCK = 2048
FIRST = 4
GROUP = 16
LANES = 128
NT = (((1,), (1,)), ((), ()))

gamma_rate = 0.03125


def run_groups():
    near = [FIRST + (low - FIRST) % ZL for low in range(ZL)]
    return [near, [(place + ZL) % (ZH * ZL) for place in near]]


def call(kernel, out_shape, *args, scratch=(), cost=None, vmem=16 << 20, space=pltpu.VMEM):
    whole = pl.BlockSpec(memory_space=pltpu.VMEM)
    several = isinstance(out_shape, tuple)
    return pl.pallas_call(
        kernel,
        in_specs=[pl.BlockSpec(memory_space=space)] * len(args),
        out_specs=(whole,) * len(out_shape) if several else whole,
        out_shape=out_shape,
        scratch_shapes=list(scratch),
        compiler_params=pltpu.CompilerParams(vmem_limit_bytes=vmem),
        cost_estimate=cost,
        name=kernel.__name__,
    )(*args)


def rounded(value):
    return value.astype(jnp.bfloat16).astype(jnp.float32)


def three_parts(value):
    high = rounded(value)
    middle = rounded(value - high)
    return high, middle, value - high - middle


def ones_kernel(out_ref):
    lane = lax.broadcasted_iota(jnp.int32, (OWN, LANES), 1) - GROUP * lax.axis_index("zl")
    out_ref[...] = jnp.where((lane >= 0) & (lane < 3), 1.0, 0.0)


def pack_kernel(land_ref, treat_ref, ones_ref, out_ref):
    land = land_ref[...].astype(jnp.float32)
    row = lax.broadcasted_iota(jnp.int32, (OWN, OWN), 0)
    col = lax.broadcasted_iota(jnp.int32, (OWN, OWN), 1)
    treat = jnp.broadcast_to(treat_ref[...].astype(jnp.float32), (OWN, OWN))
    treat = jnp.sum(jnp.where(row == col, treat, 0.0), axis=1, keepdims=True)
    own = -gamma_rate * jnp.sum(land * land, axis=1, keepdims=True) - 0.5 * treat * treat
    lane = lax.broadcasted_iota(jnp.int32, (OWN, LANES), 1) - GROUP * lax.axis_index("zl")
    extra = ones_ref[...]
    for at, part in enumerate((treat,) + three_parts(own)):
        extra = jnp.where(lane == 3 + at, part, extra)
    land = (land * (2.0 * gamma_rate)).astype(jnp.bfloat16)
    extra = extra.astype(jnp.bfloat16)
    for place in range(ZL):
        out_ref[place, :OWN] = land
        out_ref[place, OWN:] = extra


def run_kernel(run_ref, out_ref):
    extra = run_ref[0, OWN:].astype(jnp.float32)
    for place in range(1, ZL):
        extra += run_ref[place, OWN:].astype(jnp.float32)
    extra = extra.astype(jnp.bfloat16)
    for place in range(Y * X):
        for part in range(ZL):
            out_ref[place, part * OWN : (part + 1) * OWN] = run_ref[part, :OWN]
        out_ref[place, RUN:] = extra


def hide_sums(parity):
    row = lax.broadcasted_iota(jnp.int32, (RUN, LANES), 0)
    lane = lax.broadcasted_iota(jnp.int32, (RUN, LANES), 1)
    block = row // OWN == (lane - RUN * parity) // OWN
    block = block & (lane >= RUN * parity)
    at, col = row % OWN, lane % OWN
    return (
        block & (at == 7) & (col < 7),
        block & (at == 6) & (col < 6),
        block & (at == 5) & (col < 3),
    )


def half_gram(which, feat, out_ref, acc):
    per_panel = Y * X // PANELS
    size = per_panel * RUN
    half = size // CORE
    masks = [hide_sums(parity) for parity in range(LANES // RUN)]
    first_col = lax.broadcasted_iota(jnp.int32, (1, LANES), 1) % OWN == 0
    for panel in range(PANELS):
        mine = feat[panel, pl.ds(pl.multiple_of(which * half, half), half), :]
        acc[...] = lax.dot_general(feat[panel], mine, NT, preferred_element_type=jnp.float32)
        for spot in range(per_panel):
            place, first = panel * per_panel + spot, spot * RUN
            for tile in range(half // LANES):
                lanes = slice(tile * LANES, (tile + 1) * LANES)
                value = acc[first : first + RUN, lanes]
                if tile == (first % half) // LANES:
                    sums = acc[size : size + 8, lanes]
                    tail = jnp.where(
                        first_col,
                        pltpu.roll(sums, LANES - 7, 1)[0:1],
                        pltpu.roll(sums, LANES - 5, 1)[1:2],
                    )
                    hidden = value
                    for mask, part in zip(
                        masks[spot % (LANES // RUN)], (sums[0:1], sums[1:2], tail), strict=True
                    ):
                        hidden = jnp.where(mask, part, hidden)
                    value = jnp.where(which == first // half, hidden, value)
                out_ref[place, tile * RUN : (tile + 1) * RUN, :] = value.astype(out_ref.dtype)


def send_kernel(rows_ref, flag_ref, plane_ref, send_ref, feat, land, acc):
    per_panel = Y * X // PANELS
    size = per_panel * RUN
    half = size // CORE
    rows, width = rows_ref.shape
    lane = lax.broadcasted_iota(jnp.int32, (8, LANES), 1)
    for place in range(Y * X):
        panel, base = place // per_panel, (place % per_panel) * RUN
        land[panel, base : base + RUN, :LANES] = plane_ref[place, :RUN]
        packed = plane_ref[place, RUN:].astype(jnp.float32)
        pieces = []
        for group in range(ZL):
            rolled = packed if group == 0 else pltpu.roll(packed, LANES - GROUP * group, 1)
            pieces.append(jnp.where(lane < GROUP, rolled, 0.0))
        extra = jnp.concatenate(pieces, axis=0).astype(jnp.bfloat16)
        land[panel, base : base + RUN, LANES:] = extra
    ones = jnp.ones((8, 2 * width), jnp.bfloat16)
    for at in range(0, rows, BLOCK):
        block = rows_ref[at : at + BLOCK, :]
        square = jnp.square(block.astype(jnp.float32))
        high = square.astype(jnp.bfloat16)
        low = (square - high.astype(jnp.float32)).astype(jnp.bfloat16)
        total = lax.dot_general(
            ones, jnp.concatenate([high, low], axis=1), NT, preferred_element_type=jnp.float32
        )
        flag = flag_ref[0:1, at : at + BLOCK].astype(jnp.float32)
        own = three_parts(gamma_rate * (2.0 * width - total) - 0.5 * flag)
        row = lax.broadcasted_iota(jnp.int32, (8, BLOCK), 0)
        extra = jnp.where(row == 3, flag, 1.0)
        for index, part in enumerate(own):
            extra = jnp.where(row == index, part, extra)
        extra = jnp.concatenate([extra, jnp.zeros((LANES - 8, BLOCK), jnp.float32)], axis=0)
        wide = jnp.concatenate([block, extra.T.astype(jnp.bfloat16)], axis=1)
        row = lax.broadcasted_iota(jnp.int32, (MASKS, BLOCK), 0)
        mask = jnp.where(row == 0, flag, jnp.where(row == 1, 1.0 - flag, 0.0))
        for panel in range(PANELS):
            arg = lax.dot_general(land[panel], wide, NT, preferred_element_type=jnp.float32)
            feat[panel, :size, at : at + BLOCK] = jnp.exp(arg).astype(jnp.bfloat16)
            feat[panel, size:, at : at + BLOCK] = mask.astype(jnp.bfloat16)
    half_gram(1 - lax.axis_index("core"), feat, send_ref, acc)


def keep_kernel(feat, keep_ref, acc):
    half_gram(lax.axis_index("core"), feat, keep_ref, acc)


def chip_gram(rows, flag, plane):
    size = Y * X // PANELS * RUN
    half = size // CORE
    shape = (Y * X, half // LANES * RUN, LANES)
    count, width = rows.shape
    acc = pltpu.VMEM((size + MASKS, half), jnp.float32)
    flops = 2 * count * PANELS * size * half
    send, feat = call(
        send_kernel,
        (
            jax.ShapeDtypeStruct(shape, jnp.bfloat16),
            jax.ShapeDtypeStruct((PANELS, size + MASKS, count), jnp.bfloat16),
        ),
        rows,
        flag,
        plane,
        scratch=[pltpu.VMEM((PANELS, size, 2 * LANES), jnp.bfloat16), acc],
        cost=pl.CostEstimate(
            flops=flops + 4 * count * PANELS * size * width,
            transcendentals=count * PANELS * size,
            bytes_accessed=6 << 20,
        ),
        vmem=32 << 20,
    )
    got = lax.ppermute(send, "core", [(0, 1), (1, 0)])
    keep = call(
        keep_kernel,
        jax.ShapeDtypeStruct(shape, jnp.float32),
        feat,
        scratch=[acc],
        cost=pl.CostEstimate(flops=flops, transcendentals=0, bytes_accessed=6 << 20),
        vmem=16 << 20,
    )
    return got, keep


def pair_kernel(keep_ref, got_ref, out_ref):
    out_ref[...] = (keep_ref[...] + got_ref[...].astype(jnp.float32)).astype(jnp.bfloat16)


def plane_sum_kernel(terms_ref, out_ref):
    total = terms_ref[0].astype(jnp.float32)
    for place in range(1, Y * X):
        total += terms_ref[place].astype(jnp.float32)
    total = total.astype(jnp.bfloat16)
    tiles = total.shape[0] // RUN
    for high in range(ZH):
        for low in range(ZL):
            for tile in range(tiles):
                at = tile * RUN + low * OWN
                out_ref[high * ZL + low, tile * OWN : (tile + 1) * OWN] = total[at : at + OWN]


def ring_sum_kernel(terms_ref, out_ref):
    total = terms_ref[0].astype(jnp.float32)
    for place in range(1, ZH * ZL):
        total += terms_ref[place].astype(jnp.float32)
    out_ref[...] = total


def finish_kernel(scale, both_ref, treat_ref, gram_ref, moment_ref):
    tiles = both_ref.shape[0] // OWN
    for at in range(tiles):
        gram_ref[:, at * LANES : (at + 1) * LANES] = both_ref[at * OWN : (at + 1) * OWN] * scale
    y, x = lax.axis_index("y"), lax.axis_index("x")
    per_row = LANES // RUN
    spot = (y % (Y // PANELS)) * X + x
    at = spot // per_row
    shift = RUN * (spot % per_row) + OWN * lax.axis_index("zl")
    block = both_ref[pl.ds(pl.multiple_of(at * OWN, OWN), OWN), :]
    block = pltpu.roll(block, (LANES - shift) % LANES, 1)
    row = lax.broadcasted_iota(jnp.int32, (OWN, LANES), 0)
    lane = lax.broadcasted_iota(jnp.int32, (OWN, LANES), 1)
    mirror = jnp.concatenate([block, jnp.zeros((LANES - OWN, LANES), jnp.float32)], axis=0).T[:OWN]
    whole = pltpu.roll(jnp.where(lane < row, mirror, block), shift, 1)
    gram_ref[:, pl.ds(pl.multiple_of(at * LANES, LANES), LANES)] = whole * scale
    lane = lane[:1]
    sum_one = jnp.where(lane < 7, block[7:8], pltpu.roll(block, 7, 1)[5:6])
    sum_zero = jnp.where(lane < 6, block[6:7], pltpu.roll(block, 5, 1)[5:6])
    treat = treat_ref[...].astype(jnp.float32)
    on_one = jnp.exp(-0.5 * jnp.square(1.0 - treat))
    on_zero = jnp.exp(-0.5 * jnp.square(treat))
    kern = sum_one[:, :OWN] / on_one + sum_zero[:, :OWN] / on_zero
    moment_ref[...] = (on_one - on_zero) * (kern * scale)


def on_device(covariates, treated, landmarks, land_treat):
    count, width = covariates.shape
    scale = 1.0 / (count * Y * X * ZL * ZH * CORE)
    bf16, f32 = jnp.bfloat16, jnp.float32
    treat_row = land_treat.reshape(1, OWN)
    early = pl.CostEstimate(flops=1 << 32, transcendentals=0, bytes_accessed=1 << 25)
    ones = call(ones_kernel, jax.ShapeDtypeStruct((OWN, LANES), f32), cost=early)
    packed = jax.ShapeDtypeStruct((ZL, 2 * OWN, width), bf16)
    run = call(pack_kernel, packed, landmarks, treat_row, ones)
    run = lax.all_to_all(run, RING, 0, 0, axis_index_groups=run_groups())
    plane = call(
        run_kernel,
        jax.ShapeDtypeStruct((Y * X, RUN + 8, width), bf16),
        run,
        cost=early,
    )
    plane = lax.all_to_all(plane, PLANE, 0, 0)

    got, keep = chip_gram(covariates, treated.reshape(1, count), plane)
    terms = call(pair_kernel, jax.ShapeDtypeStruct(got.shape, bf16), keep, got)
    terms = lax.all_to_all(terms, PLANE, 0, 0)
    rows = terms.shape[1] // ZL
    ring = call(plane_sum_kernel, jax.ShapeDtypeStruct((ZH * ZL, rows, LANES), bf16), terms)
    ring = lax.all_to_all(ring, RING, 0, 0)
    ring = call(ring_sum_kernel, jax.ShapeDtypeStruct((rows, LANES), f32), ring)
    both = lax.all_gather(ring, "core", axis=0, tiled=True)

    def finish(*refs):
        finish_kernel(scale, *refs)

    gram, moment = call(
        finish,
        (
            jax.ShapeDtypeStruct((OWN, CORE * rows // OWN * LANES), f32),
            jax.ShapeDtypeStruct((1, OWN), f32),
        ),
        both,
        treat_row,
    )
    return gram, moment.reshape(OWN)


def solution(mesh):
    fine = Mesh(mesh.devices.reshape(Y, X, ZL, ZH, CORE), ("y", "x", "zl", "zh", "core"))
    rows, rep = ("y", "x", "zl"), ("zh", "core")
    in_specs = (P(rows + rep, None), P(rows + rep), P(rows, None), P(rows))
    out_specs = (P(rows, None), P(rows))
    return jax.shard_map(
        on_device, mesh=fine, in_specs=in_specs, out_specs=out_specs, check_vma=False
    )
```

```python
import jax
import jax.numpy as jnp
from jax import lax
from jax.experimental import pallas as pl
from jax.experimental.pallas import tpu as pltpu
from jax.sharding import Mesh, PartitionSpec as P

Y, X, ZL, ZH, CORE = 4, 4, 8, 2, 2
PLANE = ("y", "x")
RING = ("zh", "zl")
PANELS = 2
OWN = 8
RUN = ZL * OWN
MASKS = 16
BLOCK = 2048
FIRST = 4
NEAR_LEAD, RING_LEAD, PLANE_LEAD = 0, 10, 10
NEAR_ORDER = [(NEAR_LEAD + step) % ZL for step in range(ZL)]
RING_ORDER = [(RING_LEAD + step) % (ZH * ZL) for step in range(ZH * ZL)]
PLANE_ORDER = [(PLANE_LEAD + step) % (Y * X) for step in range(Y * X)]
GROUP = 16
LANES = 128
NT = (((1,), (1,)), ((), ()))

gamma_rate = 0.03125


def run_groups():
    near = [FIRST + (low - FIRST) % ZL for low in NEAR_ORDER]
    return [near, [(place + ZL) % (ZH * ZL) for place in near]]


def call(kernel, out_shape, *args, scratch=(), cost=None, vmem=16 << 20, space=pltpu.VMEM):
    whole = pl.BlockSpec(memory_space=pltpu.VMEM)
    several = isinstance(out_shape, tuple)
    return pl.pallas_call(
        kernel,
        in_specs=[pl.BlockSpec(memory_space=space)] * len(args),
        out_specs=(whole,) * len(out_shape) if several else whole,
        out_shape=out_shape,
        scratch_shapes=list(scratch),
        compiler_params=pltpu.CompilerParams(vmem_limit_bytes=vmem),
        cost_estimate=cost,
        name=kernel.__name__,
    )(*args)


def rounded(value):
    return value.astype(jnp.bfloat16).astype(jnp.float32)


def three_parts(value):
    high = rounded(value)
    middle = rounded(value - high)
    return high, middle, value - high - middle


def ones_kernel(out_ref):
    lane = lax.broadcasted_iota(jnp.int32, (OWN, LANES), 1) - GROUP * lax.axis_index("zl")
    out_ref[...] = jnp.where((lane >= 0) & (lane < 3), 1.0, 0.0)


def pack_kernel(land_ref, treat_ref, ones_ref, out_ref):
    land = land_ref[...].astype(jnp.float32)
    row = lax.broadcasted_iota(jnp.int32, (OWN, OWN), 0)
    col = lax.broadcasted_iota(jnp.int32, (OWN, OWN), 1)
    treat = jnp.broadcast_to(treat_ref[...].astype(jnp.float32), (OWN, OWN))
    treat = jnp.sum(jnp.where(row == col, treat, 0.0), axis=1, keepdims=True)
    own = -gamma_rate * jnp.sum(land * land, axis=1, keepdims=True) - 0.5 * treat * treat
    lane = lax.broadcasted_iota(jnp.int32, (OWN, LANES), 1) - GROUP * lax.axis_index("zl")
    extra = ones_ref[...]
    for at, part in enumerate((treat,) + three_parts(own)):
        extra = jnp.where(lane == 3 + at, part, extra)
    land = (land * (2.0 * gamma_rate)).astype(jnp.bfloat16)
    extra = extra.astype(jnp.bfloat16)
    for place in range(ZL):
        out_ref[place, :OWN] = land
        out_ref[place, OWN:] = extra


def run_kernel(run_ref, out_ref):
    extra = run_ref[0, OWN:].astype(jnp.float32)
    for place in range(1, ZL):
        extra += run_ref[place, OWN:].astype(jnp.float32)
    extra = extra.astype(jnp.bfloat16)
    for place in range(Y * X):
        for part in range(ZL):
            out_ref[place, part * OWN : (part + 1) * OWN] = run_ref[NEAR_ORDER.index(part), :OWN]
        out_ref[place, RUN:] = extra


def hide_sums(parity):
    row = lax.broadcasted_iota(jnp.int32, (RUN, LANES), 0)
    lane = lax.broadcasted_iota(jnp.int32, (RUN, LANES), 1)
    block = row // OWN == (lane - RUN * parity) // OWN
    block = block & (lane >= RUN * parity)
    at, col = row % OWN, lane % OWN
    return (
        block & (at == 7) & (col < 7),
        block & (at == 6) & (col < 6),
        block & (at == 5) & (col < 3),
    )


def half_gram(which, panel, feat, out_ref):
    per_panel = Y * X // PANELS
    size = per_panel * RUN
    half = size // CORE
    masks = [hide_sums(parity) for parity in range(LANES // RUN)]
    first_col = lax.broadcasted_iota(jnp.int32, (1, LANES), 1) % OWN == 0
    mine = feat[pl.ds(pl.multiple_of(which * half, half), half), :]
    gram = lax.dot_general(feat[...], mine, NT, preferred_element_type=jnp.float32)
    for spot in range(per_panel):
        place, first = PLANE_ORDER.index(panel * per_panel + spot), spot * RUN
        for tile in range(half // LANES):
            lanes = slice(tile * LANES, (tile + 1) * LANES)
            value = gram[first : first + RUN, lanes]
            if tile == (first % half) // LANES:
                sums = gram[size : size + 8, lanes]
                tail = jnp.where(
                    first_col,
                    pltpu.roll(sums, LANES - 7, 1)[0:1],
                    pltpu.roll(sums, LANES - 5, 1)[1:2],
                )
                hidden = value
                for mask, part in zip(
                    masks[spot % (LANES // RUN)], (sums[0:1], sums[1:2], tail), strict=True
                ):
                    hidden = jnp.where(mask, part, hidden)
                value = jnp.where(which == first // half, hidden, value)
            out_ref[place, tile * RUN : (tile + 1) * RUN, :] = value.astype(out_ref.dtype)


def send_kernel(rows_ref, flag_ref, plane_ref, send_ref, feat_a, feat_b, land):
    feats = (feat_a, feat_b)
    per_panel = Y * X // PANELS
    size = per_panel * RUN
    half = size // CORE
    rows, width = rows_ref.shape
    lane = lax.broadcasted_iota(jnp.int32, (8, LANES), 1)
    for at, place in enumerate(PLANE_ORDER):
        panel, base = place // per_panel, (place % per_panel) * RUN
        land[panel, base : base + RUN, :LANES] = plane_ref[at, :RUN]
        packed = plane_ref[at, RUN:].astype(jnp.float32)
        pieces = []
        for group in range(ZL):
            rolled = packed if group == 0 else pltpu.roll(packed, LANES - GROUP * group, 1)
            pieces.append(jnp.where(lane < GROUP, rolled, 0.0))
        extra = jnp.concatenate(pieces, axis=0).astype(jnp.bfloat16)
        land[panel, base : base + RUN, LANES:] = extra
    ones = jnp.ones((8, 2 * width), jnp.bfloat16)
    for at in range(0, rows, BLOCK):
        block = rows_ref[at : at + BLOCK, :]
        square = jnp.square(block.astype(jnp.float32))
        high = square.astype(jnp.bfloat16)
        low = (square - high.astype(jnp.float32)).astype(jnp.bfloat16)
        total = lax.dot_general(
            ones, jnp.concatenate([high, low], axis=1), NT, preferred_element_type=jnp.float32
        )
        flag = flag_ref[0:1, at : at + BLOCK].astype(jnp.float32)
        own = three_parts(gamma_rate * (2.0 * width - total) - 0.5 * flag)
        row = lax.broadcasted_iota(jnp.int32, (8, BLOCK), 0)
        extra = jnp.where(row == 3, flag, 1.0)
        for index, part in enumerate(own):
            extra = jnp.where(row == index, part, extra)
        extra = jnp.concatenate([extra, jnp.zeros((LANES - 8, BLOCK), jnp.float32)], axis=0)
        wide = jnp.concatenate([block, extra.T.astype(jnp.bfloat16)], axis=1)
        row = lax.broadcasted_iota(jnp.int32, (MASKS, BLOCK), 0)
        mask = jnp.where(row == 0, flag, jnp.where(row == 1, 1.0 - flag, 0.0))
        for panel in range(PANELS):
            arg = lax.dot_general(land[panel], wide, NT, preferred_element_type=jnp.float32)
            feats[panel][:size, at : at + BLOCK] = jnp.exp(arg).astype(jnp.bfloat16)
            feats[panel][size:, at : at + BLOCK] = mask.astype(jnp.bfloat16)
    for panel in range(PANELS):
        half_gram(1 - lax.axis_index("core"), panel, feats[panel], send_ref)


def keep_kernel(feat_a, feat_b, keep_ref):
    for panel, feat in enumerate((feat_a, feat_b)):
        half_gram(lax.axis_index("core"), panel, feat, keep_ref)


def chip_gram(rows, flag, plane):
    size = Y * X // PANELS * RUN
    half = size // CORE
    shape = (Y * X, half // LANES * RUN, LANES)
    count, width = rows.shape
    feat = jax.ShapeDtypeStruct((size + MASKS, count), jnp.bfloat16)
    flops = 2 * count * PANELS * size * half
    send, *feats = call(
        send_kernel,
        (jax.ShapeDtypeStruct(shape, jnp.bfloat16), feat, feat),
        rows,
        flag,
        plane,
        scratch=[pltpu.VMEM((PANELS, size, 2 * LANES), jnp.bfloat16)],
        cost=pl.CostEstimate(
            flops=flops + 4 * count * PANELS * size * width,
            transcendentals=count * PANELS * size,
            bytes_accessed=6 << 20,
        ),
        vmem=32 << 20,
    )
    got = lax.ppermute(send, "core", [(0, 1), (1, 0)])
    keep = call(
        keep_kernel,
        jax.ShapeDtypeStruct(shape, jnp.float32),
        *feats,
        cost=pl.CostEstimate(flops=flops, transcendentals=0, bytes_accessed=6 << 20),
        vmem=16 << 20,
    )
    return got, keep


def pair_kernel(keep_ref, got_ref, out_ref):
    out_ref[...] = (keep_ref[...] + got_ref[...].astype(jnp.float32)).astype(jnp.bfloat16)


def plane_sum_kernel(terms_ref, out_ref):
    total = terms_ref[0].astype(jnp.float32)
    for place in range(1, Y * X):
        total += terms_ref[place].astype(jnp.float32)
    total = total.astype(jnp.bfloat16)
    tiles = total.shape[0] // RUN
    for at, place in enumerate(RING_ORDER):
        for tile in range(tiles):
            first = tile * RUN + place % ZL * OWN
            out_ref[at, tile * OWN : (tile + 1) * OWN] = total[first : first + OWN]


def ring_sum_kernel(terms_ref, out_ref):
    total = terms_ref[0].astype(jnp.float32)
    for place in range(1, ZH * ZL):
        total += terms_ref[place].astype(jnp.float32)
    out_ref[...] = total


def finish_kernel(scale, both_ref, treat_ref, gram_ref, moment_ref):
    tiles = both_ref.shape[0] // OWN
    for at in range(tiles):
        gram_ref[:, at * LANES : (at + 1) * LANES] = both_ref[at * OWN : (at + 1) * OWN] * scale
    y, x = lax.axis_index("y"), lax.axis_index("x")
    per_row = LANES // RUN
    spot = (y % (Y // PANELS)) * X + x
    at = spot // per_row
    shift = RUN * (spot % per_row) + OWN * lax.axis_index("zl")
    block = both_ref[pl.ds(pl.multiple_of(at * OWN, OWN), OWN), :]
    block = pltpu.roll(block, (LANES - shift) % LANES, 1)
    row = lax.broadcasted_iota(jnp.int32, (OWN, LANES), 0)
    lane = lax.broadcasted_iota(jnp.int32, (OWN, LANES), 1)
    mirror = jnp.concatenate([block, jnp.zeros((LANES - OWN, LANES), jnp.float32)], axis=0).T[:OWN]
    whole = pltpu.roll(jnp.where(lane < row, mirror, block), shift, 1)
    gram_ref[:, pl.ds(pl.multiple_of(at * LANES, LANES), LANES)] = whole * scale
    lane = lane[:1]
    sum_one = jnp.where(lane < 7, block[7:8], pltpu.roll(block, 7, 1)[5:6])
    sum_zero = jnp.where(lane < 6, block[6:7], pltpu.roll(block, 5, 1)[5:6])
    treat = treat_ref[...].astype(jnp.float32)
    on_one = jnp.exp(-0.5 * jnp.square(1.0 - treat))
    on_zero = jnp.exp(-0.5 * jnp.square(treat))
    kern = sum_one[:, :OWN] / on_one + sum_zero[:, :OWN] / on_zero
    moment_ref[...] = (on_one - on_zero) * (kern * scale)


def on_device(covariates, treated, landmarks, land_treat):
    count, width = covariates.shape
    scale = 1.0 / (count * Y * X * ZL * ZH * CORE)
    bf16, f32 = jnp.bfloat16, jnp.float32
    treat_row = land_treat.reshape(1, OWN)
    early = pl.CostEstimate(flops=1 << 32, transcendentals=0, bytes_accessed=1 << 25)
    ones = call(ones_kernel, jax.ShapeDtypeStruct((OWN, LANES), f32), cost=early)
    packed = jax.ShapeDtypeStruct((ZL, 2 * OWN, width), bf16)
    run = call(pack_kernel, packed, landmarks, treat_row, ones)
    run = lax.all_to_all(run, RING, 0, 0, axis_index_groups=run_groups())
    plane = call(
        run_kernel,
        jax.ShapeDtypeStruct((Y * X, RUN + 8, width), bf16),
        run,
        cost=early,
    )
    plane = lax.all_to_all(plane, PLANE, 0, 0, axis_index_groups=[PLANE_ORDER])

    got, keep = chip_gram(covariates, treated.reshape(1, count), plane)
    terms = call(pair_kernel, jax.ShapeDtypeStruct(got.shape, bf16), keep, got)
    terms = lax.all_to_all(terms, PLANE, 0, 0, axis_index_groups=[PLANE_ORDER])
    rows = terms.shape[1] // ZL
    ring = call(plane_sum_kernel, jax.ShapeDtypeStruct((ZH * ZL, rows, LANES), bf16), terms)
    ring = lax.all_to_all(ring, RING, 0, 0, axis_index_groups=[RING_ORDER])
    ring = call(ring_sum_kernel, jax.ShapeDtypeStruct((rows, LANES), f32), ring)
    both = lax.all_gather(ring, "core", axis=0, tiled=True)

    def finish(*refs):
        finish_kernel(scale, *refs)

    gram, moment = call(
        finish,
        (
            jax.ShapeDtypeStruct((OWN, CORE * rows // OWN * LANES), f32),
            jax.ShapeDtypeStruct((1, OWN), f32),
        ),
        both,
        treat_row,
    )
    return gram, moment.reshape(OWN)


def solution(mesh):
    fine = Mesh(mesh.devices.reshape(Y, X, ZL, ZH, CORE), ("y", "x", "zl", "zh", "core"))
    rows, rep = ("y", "x", "zl"), ("zh", "core")
    in_specs = (P(rows + rep, None), P(rows + rep), P(rows, None), P(rows))
    out_specs = (P(rows, None), P(rows))
    return jax.shard_map(
        on_device, mesh=fine, in_specs=in_specs, out_specs=out_specs, check_vma=False
    )
```

```python
import jax
import jax.numpy as jnp
from jax import lax
from jax.experimental import pallas as pl
from jax.experimental.pallas import tpu as pltpu
from jax.sharding import Mesh, PartitionSpec as P

Y, X, ZL, ZH, CORE = 4, 4, 8, 2, 2
PLANE = ("y", "x")
RING = ("zh", "zl")
PANELS = 2
OWN = 8
RUN = ZL * OWN
MASKS = 16
BLOCK = 2048
FIRST = 4
NEAR_LEAD, RING_LEAD, PLANE_LEAD = 0, 9, 10
NEAR_ORDER = [(NEAR_LEAD + step) % ZL for step in range(ZL)]
RING_ORDER = [(RING_LEAD + step) % (ZH * ZL) for step in range(ZH * ZL)]
PLANE_ORDER = [(PLANE_LEAD + step) % (Y * X) for step in range(Y * X)]
GROUP = 16
LANES = 128
NT = (((1,), (1,)), ((), ()))

gamma_rate = 0.03125


def run_groups():
    near = [FIRST + (low - FIRST) % ZL for low in NEAR_ORDER]
    return [near, [(place + ZL) % (ZH * ZL) for place in near]]


def call(kernel, out_shape, *args, scratch=(), cost=None, vmem=16 << 20, space=pltpu.VMEM):
    whole = pl.BlockSpec(memory_space=pltpu.VMEM)
    several = isinstance(out_shape, tuple)
    return pl.pallas_call(
        kernel,
        in_specs=[pl.BlockSpec(memory_space=space)] * len(args),
        out_specs=(whole,) * len(out_shape) if several else whole,
        out_shape=out_shape,
        scratch_shapes=list(scratch),
        compiler_params=pltpu.CompilerParams(vmem_limit_bytes=vmem),
        cost_estimate=cost,
        name=kernel.__name__,
    )(*args)


def rounded(value):
    return value.astype(jnp.bfloat16).astype(jnp.float32)


def three_parts(value):
    high = rounded(value)
    middle = rounded(value - high)
    return high, middle, value - high - middle


def ones_kernel(out_ref):
    lane = lax.broadcasted_iota(jnp.int32, (OWN, LANES), 1) - GROUP * lax.axis_index("zl")
    out_ref[...] = jnp.where((lane >= 0) & (lane < 3), 1.0, 0.0)


def pack_kernel(land_ref, treat_ref, ones_ref, out_ref):
    land = land_ref[...].astype(jnp.float32)
    row = lax.broadcasted_iota(jnp.int32, (OWN, OWN), 0)
    col = lax.broadcasted_iota(jnp.int32, (OWN, OWN), 1)
    treat = jnp.broadcast_to(treat_ref[...].astype(jnp.float32), (OWN, OWN))
    treat = jnp.sum(jnp.where(row == col, treat, 0.0), axis=1, keepdims=True)
    own = -gamma_rate * jnp.sum(land * land, axis=1, keepdims=True) - 0.5 * treat * treat
    lane = lax.broadcasted_iota(jnp.int32, (OWN, LANES), 1) - GROUP * lax.axis_index("zl")
    extra = ones_ref[...]
    for at, part in enumerate((treat,) + three_parts(own)):
        extra = jnp.where(lane == 3 + at, part, extra)
    land = (land * (2.0 * gamma_rate)).astype(jnp.bfloat16)
    extra = extra.astype(jnp.bfloat16)
    for place in range(ZL):
        out_ref[place, :OWN] = land
        out_ref[place, OWN:] = extra


def run_kernel(run_ref, out_ref):
    extra = run_ref[0, OWN:].astype(jnp.float32)
    for place in range(1, ZL):
        extra += run_ref[place, OWN:].astype(jnp.float32)
    extra = extra.astype(jnp.bfloat16)
    for place in range(Y * X):
        for part in range(ZL):
            out_ref[place, part * OWN : (part + 1) * OWN] = run_ref[NEAR_ORDER.index(part), :OWN]
        out_ref[place, RUN:] = extra


def hide_sums(parity):
    row = lax.broadcasted_iota(jnp.int32, (RUN, LANES), 0)
    lane = lax.broadcasted_iota(jnp.int32, (RUN, LANES), 1)
    block = row // OWN == (lane - RUN * parity) // OWN
    block = block & (lane >= RUN * parity)
    at, col = row % OWN, lane % OWN
    return (
        block & (at == 7) & (col < 7),
        block & (at == 6) & (col < 6),
        block & (at == 5) & (col < 3),
    )


def half_gram(which, panel, feat, out_ref):
    per_panel = Y * X // PANELS
    size = per_panel * RUN
    half = size // CORE
    masks = [hide_sums(parity) for parity in range(LANES // RUN)]
    first_col = lax.broadcasted_iota(jnp.int32, (1, LANES), 1) % OWN == 0
    mine = feat[pl.ds(pl.multiple_of(which * half, half), half), :]
    gram = lax.dot_general(feat[...], mine, NT, preferred_element_type=jnp.float32)
    for spot in range(per_panel):
        place, first = PLANE_ORDER.index(panel * per_panel + spot), spot * RUN
        for tile in range(half // LANES):
            lanes = slice(tile * LANES, (tile + 1) * LANES)
            value = gram[first : first + RUN, lanes]
            if tile == (first % half) // LANES:
                sums = gram[size : size + 8, lanes]
                tail = jnp.where(
                    first_col,
                    pltpu.roll(sums, LANES - 7, 1)[0:1],
                    pltpu.roll(sums, LANES - 5, 1)[1:2],
                )
                hidden = value
                for mask, part in zip(
                    masks[spot % (LANES // RUN)], (sums[0:1], sums[1:2], tail), strict=True
                ):
                    hidden = jnp.where(mask, part, hidden)
                value = jnp.where(which == first // half, hidden, value)
            out_ref[place, tile * RUN : (tile + 1) * RUN, :] = value.astype(out_ref.dtype)


def send_kernel(rows_ref, flag_ref, plane_ref, send_ref, feat_a, feat_b, land):
    feats = (feat_a, feat_b)
    per_panel = Y * X // PANELS
    size = per_panel * RUN
    half = size // CORE
    rows, width = rows_ref.shape
    lane = lax.broadcasted_iota(jnp.int32, (8, LANES), 1)
    for at, place in enumerate(PLANE_ORDER):
        panel, base = place // per_panel, (place % per_panel) * RUN
        land[panel, base : base + RUN, :LANES] = plane_ref[at, :RUN]
        packed = plane_ref[at, RUN:].astype(jnp.float32)
        pieces = []
        for group in range(ZL):
            rolled = packed if group == 0 else pltpu.roll(packed, LANES - GROUP * group, 1)
            pieces.append(jnp.where(lane < GROUP, rolled, 0.0))
        extra = jnp.concatenate(pieces, axis=0).astype(jnp.bfloat16)
        land[panel, base : base + RUN, LANES:] = extra
    ones = jnp.ones((8, 2 * width), jnp.bfloat16)
    for at in range(0, rows, BLOCK):
        block = rows_ref[at : at + BLOCK, :]
        square = jnp.square(block.astype(jnp.float32))
        high = square.astype(jnp.bfloat16)
        low = (square - high.astype(jnp.float32)).astype(jnp.bfloat16)
        total = lax.dot_general(
            ones, jnp.concatenate([high, low], axis=1), NT, preferred_element_type=jnp.float32
        )
        flag = flag_ref[0:1, at : at + BLOCK].astype(jnp.float32)
        own = three_parts(gamma_rate * (2.0 * width - total) - 0.5 * flag)
        row = lax.broadcasted_iota(jnp.int32, (8, BLOCK), 0)
        extra = jnp.where(row == 3, flag, 1.0)
        for index, part in enumerate(own):
            extra = jnp.where(row == index, part, extra)
        extra = jnp.concatenate([extra, jnp.zeros((LANES - 8, BLOCK), jnp.float32)], axis=0)
        wide = jnp.concatenate([block, extra.T.astype(jnp.bfloat16)], axis=1)
        row = lax.broadcasted_iota(jnp.int32, (MASKS, BLOCK), 0)
        mask = jnp.where(row == 0, flag, jnp.where(row == 1, 1.0 - flag, 0.0))
        for panel in range(PANELS):
            arg = lax.dot_general(land[panel], wide, NT, preferred_element_type=jnp.float32)
            feats[panel][:size, at : at + BLOCK] = jnp.exp(arg).astype(jnp.bfloat16)
            feats[panel][size:, at : at + BLOCK] = mask.astype(jnp.bfloat16)
    for panel in range(PANELS):
        half_gram(1 - lax.axis_index("core"), panel, feats[panel], send_ref)


def keep_kernel(feat_a, feat_b, keep_ref):
    for panel, feat in enumerate((feat_a, feat_b)):
        half_gram(lax.axis_index("core"), panel, feat, keep_ref)


def chip_gram(rows, flag, plane):
    size = Y * X // PANELS * RUN
    half = size // CORE
    shape = (Y * X, half // LANES * RUN, LANES)
    count, width = rows.shape
    feat = jax.ShapeDtypeStruct((size + MASKS, count), jnp.bfloat16)
    flops = 2 * count * PANELS * size * half
    send, *feats = call(
        send_kernel,
        (jax.ShapeDtypeStruct(shape, jnp.bfloat16), feat, feat),
        rows,
        flag,
        plane,
        scratch=[pltpu.VMEM((PANELS, size, 2 * LANES), jnp.bfloat16)],
        cost=pl.CostEstimate(
            flops=flops + 4 * count * PANELS * size * width,
            transcendentals=count * PANELS * size,
            bytes_accessed=6 << 20,
        ),
        vmem=32 << 20,
    )
    got = lax.ppermute(send, "core", [(0, 1), (1, 0)])
    keep = call(
        keep_kernel,
        jax.ShapeDtypeStruct(shape, jnp.float32),
        *feats,
        cost=pl.CostEstimate(flops=flops, transcendentals=0, bytes_accessed=6 << 20),
        vmem=16 << 20,
    )
    return got, keep


def pair_kernel(keep_ref, got_ref, out_ref):
    out_ref[...] = (keep_ref[...] + got_ref[...].astype(jnp.float32)).astype(jnp.bfloat16)


def plane_sum_kernel(terms_ref, out_ref):
    total = terms_ref[0].astype(jnp.float32)
    for place in range(1, Y * X):
        total += terms_ref[place].astype(jnp.float32)
    total = total.astype(jnp.bfloat16)
    tiles = total.shape[0] // RUN
    for at, place in enumerate(RING_ORDER):
        for tile in range(tiles):
            first = tile * RUN + place % ZL * OWN
            out_ref[at, tile * OWN : (tile + 1) * OWN] = total[first : first + OWN]


def ring_sum_kernel(terms_ref, out_ref):
    total = terms_ref[0].astype(jnp.float32)
    for place in range(1, ZH * ZL):
        total += terms_ref[place].astype(jnp.float32)
    out_ref[...] = total


def finish_kernel(scale, both_ref, treat_ref, gram_ref, moment_ref):
    tiles = both_ref.shape[0] // OWN
    for at in range(tiles):
        gram_ref[:, at * LANES : (at + 1) * LANES] = both_ref[at * OWN : (at + 1) * OWN] * scale
    y, x = lax.axis_index("y"), lax.axis_index("x")
    per_row = LANES // RUN
    spot = (y % (Y // PANELS)) * X + x
    at = spot // per_row
    shift = RUN * (spot % per_row) + OWN * lax.axis_index("zl")
    block = both_ref[pl.ds(pl.multiple_of(at * OWN, OWN), OWN), :]
    block = pltpu.roll(block, (LANES - shift) % LANES, 1)
    row = lax.broadcasted_iota(jnp.int32, (OWN, LANES), 0)
    lane = lax.broadcasted_iota(jnp.int32, (OWN, LANES), 1)
    mirror = jnp.concatenate([block, jnp.zeros((LANES - OWN, LANES), jnp.float32)], axis=0).T[:OWN]
    whole = pltpu.roll(jnp.where(lane < row, mirror, block), shift, 1)
    gram_ref[:, pl.ds(pl.multiple_of(at * LANES, LANES), LANES)] = whole * scale
    lane = lane[:1]
    sum_one = jnp.where(lane < 7, block[7:8], pltpu.roll(block, 7, 1)[5:6])
    sum_zero = jnp.where(lane < 6, block[6:7], pltpu.roll(block, 5, 1)[5:6])
    treat = treat_ref[...].astype(jnp.float32)
    on_one = jnp.exp(-0.5 * jnp.square(1.0 - treat))
    on_zero = jnp.exp(-0.5 * jnp.square(treat))
    kern = sum_one[:, :OWN] / on_one + sum_zero[:, :OWN] / on_zero
    moment_ref[...] = (on_one - on_zero) * (kern * scale)


def on_device(covariates, treated, landmarks, land_treat):
    count, width = covariates.shape
    scale = 1.0 / (count * Y * X * ZL * ZH * CORE)
    bf16, f32 = jnp.bfloat16, jnp.float32
    treat_row = land_treat.reshape(1, OWN)
    early = pl.CostEstimate(flops=1 << 32, transcendentals=0, bytes_accessed=1 << 25)
    ones = call(ones_kernel, jax.ShapeDtypeStruct((OWN, LANES), f32), cost=early)
    packed = jax.ShapeDtypeStruct((ZL, 2 * OWN, width), bf16)
    run = call(pack_kernel, packed, landmarks, treat_row, ones)
    run = lax.all_to_all(run, RING, 0, 0, axis_index_groups=run_groups())
    plane = call(
        run_kernel,
        jax.ShapeDtypeStruct((Y * X, RUN + 8, width), bf16),
        run,
        cost=early,
    )
    plane = lax.all_to_all(plane, PLANE, 0, 0, axis_index_groups=[PLANE_ORDER])

    got, keep = chip_gram(covariates, treated.reshape(1, count), plane)
    terms = call(pair_kernel, jax.ShapeDtypeStruct(got.shape, bf16), keep, got)
    terms = lax.all_to_all(terms, PLANE, 0, 0, axis_index_groups=[PLANE_ORDER])
    rows = terms.shape[1] // ZL
    ring = call(plane_sum_kernel, jax.ShapeDtypeStruct((ZH * ZL, rows, LANES), bf16), terms)
    ring = lax.all_to_all(ring, RING, 0, 0, axis_index_groups=[RING_ORDER])
    ring = call(ring_sum_kernel, jax.ShapeDtypeStruct((rows, LANES), f32), ring)
    both = lax.all_gather(ring, "core", axis=0, tiled=True)

    def finish(*refs):
        finish_kernel(scale, *refs)

    gram, moment = call(
        finish,
        (
            jax.ShapeDtypeStruct((OWN, CORE * rows // OWN * LANES), f32),
            jax.ShapeDtypeStruct((1, OWN), f32),
        ),
        both,
        treat_row,
    )
    return gram, moment.reshape(OWN)


def solution(mesh):
    fine = Mesh(mesh.devices.reshape(Y, X, ZL, ZH, CORE), ("y", "x", "zl", "zh", "core"))
    rows, rep = ("y", "x", "zl"), ("zh", "core")
    in_specs = (P(rows + rep, None), P(rows + rep), P(rows, None), P(rows))
    out_specs = (P(rows, None), P(rows))
    return jax.shard_map(
        on_device, mesh=fine, in_specs=in_specs, out_specs=out_specs, check_vma=False
    )
```

```python
import jax
import jax.numpy as jnp
from jax import lax
from jax.experimental import pallas as pl
from jax.experimental.pallas import tpu as pltpu
from jax.sharding import Mesh, PartitionSpec as P

Y, X, ZL, ZH, CORE = 4, 4, 8, 2, 2
PLANE = ("y", "x")
RING = ("zh", "zl")
PANELS = 2
OWN = 8
RUN = ZL * OWN
MASKS = 16
BLOCK = 2048
FIRST = 5
NEAR_LEAD, RING_LEAD, PLANE_LEAD = 0, 9, 10
NEAR_ORDER = [(NEAR_LEAD + step) % ZL for step in range(ZL)]
RING_ORDER = [(RING_LEAD + step) % (ZH * ZL) for step in range(ZH * ZL)]
PLANE_ORDER = [(PLANE_LEAD + step) % (Y * X) for step in range(Y * X)]
GROUP = 16
LANES = 128
NT = (((1,), (1,)), ((), ()))

gamma_rate = 0.03125


def run_groups():
    near = [FIRST + (low - FIRST) % ZL for low in NEAR_ORDER]
    return [near, [(place + ZL) % (ZH * ZL) for place in near]]


def call(kernel, out_shape, *args, scratch=(), cost=None, vmem=16 << 20, space=pltpu.VMEM):
    whole = pl.BlockSpec(memory_space=pltpu.VMEM)
    several = isinstance(out_shape, tuple)
    return pl.pallas_call(
        kernel,
        in_specs=[pl.BlockSpec(memory_space=space)] * len(args),
        out_specs=(whole,) * len(out_shape) if several else whole,
        out_shape=out_shape,
        scratch_shapes=list(scratch),
        compiler_params=pltpu.CompilerParams(vmem_limit_bytes=vmem),
        cost_estimate=cost,
        name=kernel.__name__,
    )(*args)


def rounded(value):
    return value.astype(jnp.bfloat16).astype(jnp.float32)


def three_parts(value):
    high = rounded(value)
    middle = rounded(value - high)
    return high, middle, value - high - middle


def ones_kernel(out_ref):
    lane = lax.broadcasted_iota(jnp.int32, (OWN, LANES), 1) - GROUP * lax.axis_index("zl")
    out_ref[...] = jnp.where((lane >= 0) & (lane < 3), 1.0, 0.0)


def pack_kernel(land_ref, treat_ref, ones_ref, out_ref):
    land = land_ref[...].astype(jnp.float32)
    row = lax.broadcasted_iota(jnp.int32, (OWN, OWN), 0)
    col = lax.broadcasted_iota(jnp.int32, (OWN, OWN), 1)
    treat = jnp.broadcast_to(treat_ref[...].astype(jnp.float32), (OWN, OWN))
    treat = jnp.sum(jnp.where(row == col, treat, 0.0), axis=1, keepdims=True)
    own = -gamma_rate * jnp.sum(land * land, axis=1, keepdims=True) - 0.5 * treat * treat
    lane = lax.broadcasted_iota(jnp.int32, (OWN, LANES), 1) - GROUP * lax.axis_index("zl")
    extra = ones_ref[...]
    for at, part in enumerate((treat,) + three_parts(own)):
        extra = jnp.where(lane == 3 + at, part, extra)
    land = (land * (2.0 * gamma_rate)).astype(jnp.bfloat16)
    extra = extra.astype(jnp.bfloat16)
    for place in range(ZL):
        out_ref[place, :OWN] = land
        out_ref[place, OWN:] = extra


def run_kernel(run_ref, out_ref):
    extra = run_ref[0, OWN:].astype(jnp.float32)
    for place in range(1, ZL):
        extra += run_ref[place, OWN:].astype(jnp.float32)
    extra = extra.astype(jnp.bfloat16)
    for place in range(Y * X):
        for part in range(ZL):
            out_ref[place, part * OWN : (part + 1) * OWN] = run_ref[NEAR_ORDER.index(part), :OWN]
        out_ref[place, RUN:] = extra


def hide_sums(parity):
    row = lax.broadcasted_iota(jnp.int32, (RUN, LANES), 0)
    lane = lax.broadcasted_iota(jnp.int32, (RUN, LANES), 1)
    block = row // OWN == (lane - RUN * parity) // OWN
    block = block & (lane >= RUN * parity)
    at, col = row % OWN, lane % OWN
    return (
        block & (at == 7) & (col < 7),
        block & (at == 6) & (col < 6),
        block & (at == 5) & (col < 3),
    )


def half_gram(which, panel, feat, out_ref):
    per_panel = Y * X // PANELS
    size = per_panel * RUN
    half = size // CORE
    masks = [hide_sums(parity) for parity in range(LANES // RUN)]
    first_col = lax.broadcasted_iota(jnp.int32, (1, LANES), 1) % OWN == 0
    mine = feat[pl.ds(pl.multiple_of(which * half, half), half), :]
    gram = lax.dot_general(feat[...], mine, NT, preferred_element_type=jnp.float32)
    for spot in range(per_panel):
        place, first = PLANE_ORDER.index(panel * per_panel + spot), spot * RUN
        for tile in range(half // LANES):
            lanes = slice(tile * LANES, (tile + 1) * LANES)
            value = gram[first : first + RUN, lanes]
            if tile == (first % half) // LANES:
                sums = gram[size : size + 8, lanes]
                tail = jnp.where(
                    first_col,
                    pltpu.roll(sums, LANES - 7, 1)[0:1],
                    pltpu.roll(sums, LANES - 5, 1)[1:2],
                )
                hidden = value
                for mask, part in zip(
                    masks[spot % (LANES // RUN)], (sums[0:1], sums[1:2], tail), strict=True
                ):
                    hidden = jnp.where(mask, part, hidden)
                value = jnp.where(which == first // half, hidden, value)
            out_ref[place, tile * RUN : (tile + 1) * RUN, :] = value.astype(out_ref.dtype)


def send_kernel(rows_ref, flag_ref, plane_ref, send_ref, feat_a, feat_b, land):
    feats = (feat_a, feat_b)
    per_panel = Y * X // PANELS
    size = per_panel * RUN
    half = size // CORE
    rows, width = rows_ref.shape
    lane = lax.broadcasted_iota(jnp.int32, (8, LANES), 1)
    for at, place in enumerate(PLANE_ORDER):
        panel, base = place // per_panel, (place % per_panel) * RUN
        land[panel, base : base + RUN, :LANES] = plane_ref[at, :RUN]
        packed = plane_ref[at, RUN:].astype(jnp.float32)
        pieces = []
        for group in range(ZL):
            rolled = packed if group == 0 else pltpu.roll(packed, LANES - GROUP * group, 1)
            pieces.append(jnp.where(lane < GROUP, rolled, 0.0))
        extra = jnp.concatenate(pieces, axis=0).astype(jnp.bfloat16)
        land[panel, base : base + RUN, LANES:] = extra
    ones = jnp.ones((8, 2 * width), jnp.bfloat16)
    for at in range(0, rows, BLOCK):
        block = rows_ref[at : at + BLOCK, :]
        square = jnp.square(block.astype(jnp.float32))
        high = square.astype(jnp.bfloat16)
        low = (square - high.astype(jnp.float32)).astype(jnp.bfloat16)
        total = lax.dot_general(
            ones, jnp.concatenate([high, low], axis=1), NT, preferred_element_type=jnp.float32
        )
        flag = flag_ref[0:1, at : at + BLOCK].astype(jnp.float32)
        own = three_parts(gamma_rate * (2.0 * width - total) - 0.5 * flag)
        row = lax.broadcasted_iota(jnp.int32, (8, BLOCK), 0)
        extra = jnp.where(row == 3, flag, 1.0)
        for index, part in enumerate(own):
            extra = jnp.where(row == index, part, extra)
        extra = jnp.concatenate([extra, jnp.zeros((LANES - 8, BLOCK), jnp.float32)], axis=0)
        wide = jnp.concatenate([block, extra.T.astype(jnp.bfloat16)], axis=1)
        row = lax.broadcasted_iota(jnp.int32, (MASKS, BLOCK), 0)
        mask = jnp.where(row == 0, flag, jnp.where(row == 1, 1.0 - flag, 0.0))
        for panel in range(PANELS):
            arg = lax.dot_general(land[panel], wide, NT, preferred_element_type=jnp.float32)
            feats[panel][:size, at : at + BLOCK] = jnp.exp(arg).astype(jnp.bfloat16)
            feats[panel][size:, at : at + BLOCK] = mask.astype(jnp.bfloat16)
    for panel in range(PANELS):
        half_gram(1 - lax.axis_index("core"), panel, feats[panel], send_ref)


def keep_kernel(feat_a, feat_b, keep_ref):
    for panel, feat in enumerate((feat_a, feat_b)):
        half_gram(lax.axis_index("core"), panel, feat, keep_ref)


def chip_gram(rows, flag, plane):
    size = Y * X // PANELS * RUN
    half = size // CORE
    shape = (Y * X, half // LANES * RUN, LANES)
    count, width = rows.shape
    feat = jax.ShapeDtypeStruct((size + MASKS, count), jnp.bfloat16)
    flops = 2 * count * PANELS * size * half
    send, *feats = call(
        send_kernel,
        (jax.ShapeDtypeStruct(shape, jnp.bfloat16), feat, feat),
        rows,
        flag,
        plane,
        scratch=[pltpu.VMEM((PANELS, size, 2 * LANES), jnp.bfloat16)],
        cost=pl.CostEstimate(
            flops=flops + 4 * count * PANELS * size * width,
            transcendentals=count * PANELS * size,
            bytes_accessed=6 << 20,
        ),
        vmem=32 << 20,
    )
    got = lax.ppermute(send, "core", [(0, 1), (1, 0)])
    keep = call(
        keep_kernel,
        jax.ShapeDtypeStruct(shape, jnp.float32),
        *feats,
        cost=pl.CostEstimate(flops=flops, transcendentals=0, bytes_accessed=6 << 20),
        vmem=16 << 20,
    )
    return got, keep


def pair_kernel(keep_ref, got_ref, out_ref):
    out_ref[...] = (keep_ref[...] + got_ref[...].astype(jnp.float32)).astype(jnp.bfloat16)


def plane_sum_kernel(terms_ref, out_ref):
    total = terms_ref[0].astype(jnp.float32)
    for place in range(1, Y * X):
        total += terms_ref[place].astype(jnp.float32)
    total = total.astype(jnp.bfloat16)
    tiles = total.shape[0] // RUN
    for at, place in enumerate(RING_ORDER):
        for tile in range(tiles):
            first = tile * RUN + place % ZL * OWN
            out_ref[at, tile * OWN : (tile + 1) * OWN] = total[first : first + OWN]


def ring_sum_kernel(terms_ref, out_ref):
    total = terms_ref[0].astype(jnp.float32)
    for place in range(1, ZH * ZL):
        total += terms_ref[place].astype(jnp.float32)
    out_ref[...] = total


def finish_kernel(scale, both_ref, treat_ref, gram_ref, moment_ref):
    tiles = both_ref.shape[0] // OWN
    for at in range(tiles):
        gram_ref[:, at * LANES : (at + 1) * LANES] = both_ref[at * OWN : (at + 1) * OWN] * scale
    y, x = lax.axis_index("y"), lax.axis_index("x")
    per_row = LANES // RUN
    spot = (y % (Y // PANELS)) * X + x
    at = spot // per_row
    shift = RUN * (spot % per_row) + OWN * lax.axis_index("zl")
    block = both_ref[pl.ds(pl.multiple_of(at * OWN, OWN), OWN), :]
    block = pltpu.roll(block, (LANES - shift) % LANES, 1)
    row = lax.broadcasted_iota(jnp.int32, (OWN, LANES), 0)
    lane = lax.broadcasted_iota(jnp.int32, (OWN, LANES), 1)
    mirror = jnp.concatenate([block, jnp.zeros((LANES - OWN, LANES), jnp.float32)], axis=0).T[:OWN]
    whole = pltpu.roll(jnp.where(lane < row, mirror, block), shift, 1)
    gram_ref[:, pl.ds(pl.multiple_of(at * LANES, LANES), LANES)] = whole * scale
    lane = lane[:1]
    sum_one = jnp.where(lane < 7, block[7:8], pltpu.roll(block, 7, 1)[5:6])
    sum_zero = jnp.where(lane < 6, block[6:7], pltpu.roll(block, 5, 1)[5:6])
    treat = treat_ref[...].astype(jnp.float32)
    on_one = jnp.exp(-0.5 * jnp.square(1.0 - treat))
    on_zero = jnp.exp(-0.5 * jnp.square(treat))
    kern = sum_one[:, :OWN] / on_one + sum_zero[:, :OWN] / on_zero
    moment_ref[...] = (on_one - on_zero) * (kern * scale)


def on_device(covariates, treated, landmarks, land_treat):
    count, width = covariates.shape
    scale = 1.0 / (count * Y * X * ZL * ZH * CORE)
    bf16, f32 = jnp.bfloat16, jnp.float32
    treat_row = land_treat.reshape(1, OWN)
    early = pl.CostEstimate(flops=1 << 32, transcendentals=0, bytes_accessed=1 << 25)
    ones = call(ones_kernel, jax.ShapeDtypeStruct((OWN, LANES), f32), cost=early)
    packed = jax.ShapeDtypeStruct((ZL, 2 * OWN, width), bf16)
    run = call(pack_kernel, packed, landmarks, treat_row, ones)
    run = lax.all_to_all(run, RING, 0, 0, axis_index_groups=run_groups())
    plane = call(
        run_kernel,
        jax.ShapeDtypeStruct((Y * X, RUN + 8, width), bf16),
        run,
        cost=early,
    )
    plane = lax.all_to_all(plane, PLANE, 0, 0, axis_index_groups=[PLANE_ORDER])

    got, keep = chip_gram(covariates, treated.reshape(1, count), plane)
    terms = call(pair_kernel, jax.ShapeDtypeStruct(got.shape, bf16), keep, got)
    terms = lax.all_to_all(terms, PLANE, 0, 0, axis_index_groups=[PLANE_ORDER])
    rows = terms.shape[1] // ZL
    ring = call(plane_sum_kernel, jax.ShapeDtypeStruct((ZH * ZL, rows, LANES), bf16), terms)
    ring = lax.all_to_all(ring, RING, 0, 0, axis_index_groups=[RING_ORDER])
    ring = call(ring_sum_kernel, jax.ShapeDtypeStruct((rows, LANES), f32), ring)
    both = lax.all_gather(ring, "core", axis=0, tiled=True)

    def finish(*refs):
        finish_kernel(scale, *refs)

    gram, moment = call(
        finish,
        (
            jax.ShapeDtypeStruct((OWN, CORE * rows // OWN * LANES), f32),
            jax.ShapeDtypeStruct((1, OWN), f32),
        ),
        both,
        treat_row,
    )
    return gram, moment.reshape(OWN)


def solution(mesh):
    fine = Mesh(mesh.devices.reshape(Y, X, ZL, ZH, CORE), ("y", "x", "zl", "zh", "core"))
    rows, rep = ("y", "x", "zl"), ("zh", "core")
    in_specs = (P(rows + rep, None), P(rows + rep), P(rows, None), P(rows))
    out_specs = (P(rows, None), P(rows))
    return jax.shard_map(
        on_device, mesh=fine, in_specs=in_specs, out_specs=out_specs, check_vma=False
    )
```
